256 devices in a mesh: section: 8 (over z), expert: 32 (over y, x, core).
Axes of the slice: x: 4, y: 4, z: 8, core: 2. Of those that a mesh axis runs over, the one named last changes fastest.
Arguments:
- activations: bfloat16 [8, 4096, 2048], P('section', 'expert'), may hold values from -6 to 6
- gradients: bfloat16 [8, 4096, 2048], P('section', 'expert'), may hold values from -6 to 6
- stashed: bfloat16 [8, 4096, 2048], P('section', 'expert'), may hold values from -6 to 6
- norm_gain: bfloat16 [8, 2048], P('section'), may hold values from 0.5 to 1.5
- router: bfloat16 [8, 2048, 32], P('section'), may hold values from -0.125 to 0.125
- gate_weight: bfloat16 [8, 32, 2048, 768], P('section', 'expert'), may hold values from -0.125 to 0.125
- up_weight: bfloat16 [8, 32, 2048, 768], P('section', 'expert'), may hold values from -0.125 to 0.125
- down_weight: bfloat16 [8, 32, 768, 2048], P('section', 'expert'), may hold values from -0.21875 to 0.21875
- routes_forward: int32 [8, 4096, 2], P('section', 'expert'), may hold values from 0 to 31, all different within a row; in each aligned block of 128 rows (0 to 127, 128 to 255, ..., all dimensions but the last counted through in order) at most 12 rows name the same one
- routes_backward: int32 [8, 4096, 2], P('section', 'expert'), may hold values from 0 to 31, all different within a row; in each aligned block of 128 rows (0 to 127, 128 to 255, ..., all dimensions but the last counted through in order) at most 12 rows name the same one
Outputs:
- layer_out: bfloat16 [8, 4096, 2048], P('section', 'expert')
- input_grad: bfloat16 [8, 4096, 2048], P('section', 'expert')
The draws below stay inside these ranges and needn't reach their ends.
Inputs may be any that keep to these rules, and one draw needn't show every extreme that they name: `routes_forward`: each token names 2 different experts. In each aligned block of 128 tokens (one index of expert's tokens of one section) no expert is named by more than 12 tokens, a bound that some block reaches. `routes_backward`: each token names 2 different experts. In each aligned block of 128 tokens (one index of expert's tokens of one section) no expert is named by more than 12 tokens, a bound that some block reaches.
All inputs are finite; a program needn't handle non-finite values.
Results may differ from the reference program's by a relative error of at most 0.0059.
Values may be sent and summed in bfloat16 or wider, within the bound.
No kernel may reach another device: no remote copies, remote signals or barrier semaphores. Data moves between devices by JAX's collectives and lax.ppermute only.
A program may use at most 128 MiB of HBM per device.

```python
import math
from functools import partial
import jax
import jax.numpy as jnp
import numpy as np
from jax import lax

D = 2048
FF = 768
TOPK = 2
TOK_DEV = 128
SECTIONS = 8
EXPERTS = 32
TOKENS = 4096
CAP = 12
N_EXPERT = 32


def levels(key, shape, cuts, smallest, high):
    def one(axis_at, shards_of):
        draws = jax.random.uniform(jax.random.fold_in(jax.random.fold_in(key, 6), axis_at), (shards_of,), jnp.float32, smallest / len(cuts), high / len(cuts))
        return jnp.repeat(jnp.exp(draws), shape[axis_at] // shards_of).reshape((-1,) + (1,) * (len(shape) - axis_at - 1))

    gain = one(*cuts[0])
    for cut in cuts[1:]:
        gain = gain * one(*cut)
    return gain


def deal_out(stream_key, own, number, rows, count, top, limit, lean):
    ranking = jax.random.permutation(stream_key, count)
    crowded, common = shares(count, rows * top, limit, lean, True), shares(count, rows * top, limit, lean, False)
    places = jnp.arange(count)

    def named(tallies, offset_by):
        used = int((tallies > 0).sum())
        fixed = max(1, used // 4)
        passed = fixed + (places - fixed + offset_by * (used - fixed)) % max(1, count - fixed)
        return jnp.zeros((count,), jnp.int32).at[ranking[jnp.where(places < fixed, places, passed)]].set(jnp.asarray(tallies, jnp.int32))

    tallies = jnp.where(number % 4 == 0, named(crowded, number // 4), named(common, number - number // 4 - 1))
    mixed = jax.random.permutation(jax.random.fold_in(own, 3), count)
    source_of, sink = mixed[0:count // 2 * 2:2], mixed[1:count // 2 * 2:2]
    slack = jnp.minimum(tallies[source_of] - 1, limit - tallies[sink]) // 2
    slack = jnp.where((source_of == ranking[0]) | (sink == ranking[0]) | (tallies[sink] == 0), 0, jnp.maximum(slack, 0))
    passed = jax.random.randint(jax.random.fold_in(own, 4), (count // 2,), 0, 1 << 20) % (slack + 1)
    tallies = tallies.at[source_of].add(-passed).at[sink].add(passed)
    items = jnp.searchsorted(jnp.cumsum(tallies), jnp.arange(rows * top), side="right").astype(jnp.int32)
    grid = items.reshape(top, rows).T
    grid = grid[jax.random.permutation(jax.random.fold_in(own, 1), rows)]
    offset_by = jax.random.randint(jax.random.fold_in(own, 2), (rows, 1), 0, top)
    return jnp.take_along_axis(grid, (jnp.arange(top)[None, :] + offset_by) % top, axis=1)


def shares(count, total, most, skew, full):
    portions = [(1 << 20) // math.isqrt(rank ** skew) + 1 for rank in range(1, count + 1)]
    largest = most if full else min(most, max(-(-total // count), total * portions[0] // sum(portions)))
    least = 1 if total - largest >= count - 1 else 0
    holding, spare = [largest] + [least] * (count - 1), total - largest - least * (count - 1)
    while spare > 0:
        free = [i for i in range(1, count) if holding[i] < largest] or [i for i in range(1, count) if holding[i] < most]
        whole, left = sum([portions[i] for i in free]), spare
        for i in free:
            more = min(most - holding[i], max(1, left * portions[i] // whole), spare)
            holding[i] = holding[i] + more
            spare = spare - more
    return np.array(holding)


def centred(key, shape, scale, most, split=(), kind=jnp.bfloat16):
    values = jax.random.normal(key, shape, jnp.float32) * scale
    if len(split) > 0:
        values = levels(key, shape, split, -0.22, 0.18) * values
    return jnp.clip(values, min=-most, max=most).astype(kind)


def setup_inputs(seed: int = 0) -> dict:
    keys = jax.random.split(jax.random.key(seed), 11)
    activations = centred(keys[0], (SECTIONS, TOKENS, D), 1.0, 6.0, ((0, 8), (1, 32)))
    gradients = centred(keys[1], (SECTIONS, TOKENS, D), 1.0, 6.0, ((0, 8), (1, 32)))
    stashed = centred(keys[2], (SECTIONS, TOKENS, D), 1.0, 6.0, ((0, 8), (1, 32)))
    norm_gain = jnp.clip(1.0 + 0.1 * jax.random.normal(keys[3], (SECTIONS, D), jnp.float32), 0.5, 1.5).astype(jnp.bfloat16)
    router = centred(keys[4], (SECTIONS, D, EXPERTS), D ** -0.5, 0.125, ((0, 8),))
    gate_weight = centred(keys[5], (SECTIONS, EXPERTS, D, FF), D ** -0.5, 0.125, ((0, 8), (1, 32)))
    up_weight = centred(keys[6], (SECTIONS, EXPERTS, D, FF), D ** -0.5, 0.125, ((0, 8), (1, 32)))
    down_weight = centred(keys[7], (SECTIONS, EXPERTS, FF, D), FF ** -0.5, 0.21875, ((0, 8), (1, 32)))
    routes_forward_keys = jax.random.split(jax.random.fold_in(keys[8], 1), SECTIONS * TOKENS // TOK_DEV)
    routes_forward_turns = jax.random.permutation(jax.random.fold_in(keys[8], 3), SECTIONS * TOKENS // TOK_DEV)
    routes_forward = jax.vmap(lambda own, number: deal_out(jax.random.fold_in(keys[8], 2), own, number, TOK_DEV, EXPERTS, TOPK, CAP, 2))(routes_forward_keys, routes_forward_turns).reshape((SECTIONS, TOKENS, TOPK))
    routes_backward_keys = jax.random.split(jax.random.fold_in(keys[9], 1), SECTIONS * TOKENS // TOK_DEV)
    routes_backward_turns = jax.random.permutation(jax.random.fold_in(keys[9], 3), SECTIONS * TOKENS // TOK_DEV)
    routes_backward = jax.vmap(lambda own, number: deal_out(jax.random.fold_in(keys[9], 2), own, number, TOK_DEV, EXPERTS, TOPK, CAP, 2))(routes_backward_keys, routes_backward_turns).reshape((SECTIONS, TOKENS, TOPK))
    return {"activations": activations, "gradients": gradients, "stashed": stashed, "norm_gain": norm_gain, "router": router, "gate_weight": gate_weight, "up_weight": up_weight, "down_weight": down_weight, "routes_forward": routes_forward, "routes_backward": routes_backward}


NORM_EPS = 1e-06

def normalize(tokens, gain_row):
    values = tokens.astype(jnp.float32)
    inverse = lax.rsqrt(lax.optimization_barrier(jnp.mean(values * values, axis=-1, keepdims=True)) + NORM_EPS)
    normed = (values * inverse * gain_row.astype(jnp.float32)).astype(jnp.bfloat16)
    return (normed, inverse)

def route_weights(normed, router_mat, routes):
    logits = jnp.dot(normed, router_mat, preferred_element_type=jnp.float32)
    columns = jnp.arange(router_mat.shape[1], dtype=jnp.int32)
    matches = (routes[:, :, None] == columns[None, None, :]).astype(jnp.float32)
    picked = lax.optimization_barrier(jnp.sum(matches * logits[:, None, :], axis=2))
    sigmoids = jax.nn.sigmoid(picked)
    totals = lax.optimization_barrier(jnp.sum(sigmoids, axis=1, keepdims=True))
    return (sigmoids / totals, sigmoids, totals, matches)

def slot_positions(routes, expert_count, capacity):
    columns = jnp.arange(expert_count, dtype=jnp.int32)
    matches = (routes[:, :, None] == columns[None, None, :]).astype(jnp.int32)
    per_row = lax.optimization_barrier(jnp.sum(matches, axis=1))
    earlier = jnp.cumsum(per_row, axis=0) - per_row
    slots = lax.optimization_barrier(jnp.sum(matches * earlier[:, None, :], axis=2))
    return (routes * capacity + slots).astype(jnp.int32)

def dispatch_table(position, scales, slot_count):
    targets = jnp.arange(slot_count, dtype=jnp.int32)
    matches = position[None, :, :] == targets[:, None, None]
    return lax.optimization_barrier(jnp.sum(jnp.where(matches, scales[None, :, :], 0.0), axis=2)).astype(jnp.bfloat16)

def expert_forward(slot_rows, gate_mat, up_mat, down_mat):
    gate = jnp.dot(slot_rows, gate_mat, preferred_element_type=jnp.float32)
    upper = jnp.dot(slot_rows, up_mat, preferred_element_type=jnp.float32)
    hidden = (jax.nn.silu(gate) * upper).astype(jnp.bfloat16)
    result = jnp.dot(hidden, down_mat, preferred_element_type=jnp.float32).astype(jnp.bfloat16)
    return (result, gate, upper)

def expert_backward(slot_rows, slot_grad, gate_mat, up_mat, down_mat):
    result, gate, upper = expert_forward(slot_rows, gate_mat, up_mat, down_mat)
    dims = (((1,), (1,)), ((), ()))
    grad_hidden = lax.dot_general(slot_grad, down_mat, dims, preferred_element_type=jnp.float32)
    sigmoid_gate = jax.nn.sigmoid(gate)
    grad_up = (grad_hidden * gate * sigmoid_gate).astype(jnp.bfloat16)
    grad_gate = (grad_hidden * upper * sigmoid_gate * (1.0 + gate * (1.0 - sigmoid_gate))).astype(jnp.bfloat16)
    row_grad = lax.dot_general(grad_gate, gate_mat, dims, preferred_element_type=jnp.float32)
    row_grad = row_grad + lax.dot_general(grad_up, up_mat, dims, preferred_element_type=jnp.float32)
    return (result, row_grad.astype(jnp.bfloat16))

def router_backward(scores, weights, sigmoids, totals, matches, router_mat):
    mixed_score = lax.optimization_barrier(jnp.sum(weights * scores, axis=1, keepdims=True))
    grad_pick = (scores - mixed_score) / totals * sigmoids * (1.0 - sigmoids)
    grad_logits = lax.optimization_barrier(jnp.sum(grad_pick[:, :, None] * matches, axis=1))
    return jnp.dot(grad_logits, router_mat.astype(jnp.float32).T, precision=lax.Precision.HIGHEST)

def norm_backward(tokens, inverse, gain_row, grad_normed):
    values = tokens.astype(jnp.float32)
    grad_pre = grad_normed * gain_row.astype(jnp.float32)
    cubed = inverse * inverse * inverse
    return inverse * grad_pre - values * cubed * lax.optimization_barrier(jnp.mean(grad_pre * values, axis=-1, keepdims=True))

def forward_only(operands):
    slot_rows, gate_mat, up_mat, down_mat = operands
    return expert_forward(slot_rows, gate_mat, up_mat, down_mat)[0]

def backward_only(operands):
    slot_rows, slot_grad, gate_mat, up_mat, down_mat = operands
    return expert_backward(slot_rows, slot_grad, gate_mat, up_mat, down_mat)

def section_pass(operands):
    arrived, stored, cotangent, gain_row, router_mat, gate_all, up_all, down_all, route_front, route_back = operands
    sources = N_EXPERT
    experts = gate_all.shape[0]
    capacity = CAP
    slot_count = experts * capacity
    model_width = arrived.shape[1]
    per_source = arrived.shape[0] // sources

    def to_experts(buffers):
        shaped = buffers.reshape(sources, experts, capacity, model_width)
        return shaped.transpose(1, 0, 2, 3).reshape(experts, sources * capacity, model_width)

    def from_experts(outputs):
        shaped = outputs.reshape(experts, sources, capacity, model_width)
        return shaped.transpose(1, 0, 2, 3).reshape(sources, slot_count, model_width)

    def gather_slots(returned, position):
        picked = jax.vmap(partial(jnp.take, axis=0))(returned, position)
        return picked.reshape(sources * per_source, -1, model_width)

    def fill_slots(position, scales, tokens):
        tables = jax.vmap(partial(dispatch_table, slot_count=slot_count))(position, scales)
        grouped = tokens.reshape(sources, per_source, model_width)
        filled = jnp.einsum('njr,nrd->njd', tables.astype(jnp.float32), grouped.astype(jnp.float32))
        return filled.astype(jnp.bfloat16)
    locate = jax.vmap(partial(slot_positions, expert_count=experts, capacity=capacity))
    normed_f, inverse_f = normalize(arrived, gain_row)
    weights_f, sig_f, tot_f, match_f = route_weights(normed_f, router_mat, route_front)
    position_f = locate(route_front.reshape(sources, per_source, -1))
    unit_scales = jnp.ones(position_f.shape, jnp.float32)
    buffer_f = fill_slots(position_f, unit_scales, normed_f)
    outputs_f = lax.map(forward_only, (to_experts(buffer_f), gate_all, up_all, down_all))
    picked_f = gather_slots(from_experts(outputs_f), position_f)
    combined = lax.optimization_barrier(jnp.sum(weights_f[:, :, None] * picked_f.astype(jnp.float32), axis=1))
    layer_out = (arrived.astype(jnp.float32) + combined).astype(jnp.bfloat16)
    normed_b, inverse_b = normalize(stored, gain_row)
    weights_b, sig_b, tot_b, match_b = route_weights(normed_b, router_mat, route_back)
    position_b = locate(route_back.reshape(sources, per_source, -1))
    scale_round = lax.optimization_barrier(weights_b.astype(jnp.bfloat16)).astype(jnp.float32)
    buffer_b = fill_slots(position_b, unit_scales, normed_b)
    grad_buffer = fill_slots(position_b, scale_round.reshape(sources, per_source, -1), cotangent)
    outputs_b, grads_b = lax.map(backward_only, (to_experts(buffer_b), to_experts(grad_buffer), gate_all, up_all, down_all))
    picked_o = gather_slots(from_experts(outputs_b), position_b)
    picked_dn = gather_slots(from_experts(grads_b), position_b)
    scores = lax.optimization_barrier(jnp.sum(picked_o.astype(jnp.float32) * cotangent.astype(jnp.float32)[:, None, :], axis=2))
    scores = lax.optimization_barrier(scores.astype(jnp.bfloat16)).astype(jnp.float32)
    grad_normed = lax.optimization_barrier(jnp.sum(picked_dn.astype(jnp.float32), axis=1))
    grad_normed = grad_normed + router_backward(scores, weights_b, sig_b, tot_b, match_b, router_mat)
    input_grad = cotangent.astype(jnp.float32) + norm_backward(stored, inverse_b, gain_row, grad_normed)
    return (layer_out, input_grad.astype(jnp.bfloat16))

def reference(activations, gradients, stashed, norm_gain, router, gate_weight, up_weight, down_weight, routes_forward, routes_backward):
    arrived = jnp.roll(activations, 1, axis=0)
    cotangents = jnp.roll(gradients, -1, axis=0)
    layer_out, input_grad = lax.map(section_pass, (arrived, stashed, cotangents, norm_gain, router, gate_weight, up_weight, down_weight, routes_forward, routes_backward))
    return (layer_out, input_grad)
```

```python
import functools

import jax
import jax.numpy as jnp
from jax import lax
from jax.experimental import pallas as pl
from jax.experimental.pallas import tpu as pltpu
from jax.sharding import PartitionSpec as P

NORM_EPS = 1e-06
LOW = 8
HIGH = 4
F32 = jnp.float32
BF16 = jnp.bfloat16
NT = (((1,), (1,)), ((), ()))


def passed_along(value, axis, steps):
    count = lax.axis_size(axis)
    pairs = [(source, (source + steps) % count) for source in range(count)]
    return lax.ppermute(value, axis, pairs)


def mm(a, b):
    return jnp.dot(a, b, preferred_element_type=F32)


def mm_nt(a, b):
    return lax.dot_general(a, b, NT, preferred_element_type=F32)


def iota(shape, dim):
    return lax.broadcasted_iota(jnp.int32, shape, dim)


def normalized(tokens, gain_row):
    values = tokens.astype(F32)
    inverse = lax.rsqrt(jnp.mean(values * values, axis=-1, keepdims=True) + NORM_EPS)
    return (values * inverse * gain_row.astype(F32)).astype(BF16), inverse


def places(routes, experts):
    rows = routes.shape[0]
    columns = iota((rows, experts), 1)
    matches = [routes[:, k : k + 1] == columns for k in range(2)]
    named = jnp.where(matches[0] | matches[1], 1.0, 0.0).astype(BF16)
    before = (iota((rows, rows), 0) > iota((rows, rows), 1)).astype(F32).astype(BF16)
    earlier = mm(before, named)
    found = []
    for k in range(2):
        slot = jnp.sum(jnp.where(matches[k], earlier, 0.0), axis=1, keepdims=True).astype(jnp.int32)
        base = routes[:, k : k + 1] * LOW
        whole = jnp.where(slot < LOW, base + slot, -LOW)
        half = jnp.where(slot < LOW, -LOW, base + slot - LOW)
        found.append((whole, half, matches[k]))
    return found


def table(lanes, spots, scales):
    total = jnp.where(lanes == spots[0], scales[0], 0.0)
    return total + jnp.where(lanes == spots[1], scales[1], 0.0)


def pack(tokens, whole, left, right, out_ref, at):
    width = tokens.shape[1]
    half = width // 2
    out_ref[:, at : at + width] = mm(whole.T.astype(BF16), tokens).astype(BF16)
    both = mm(left.T.astype(BF16), tokens[:, :half]) + mm(right.T.astype(BF16), tokens[:, half:])
    out_ref[:, at + width : at + width + half] = both.astype(BF16)


def pack_stored(stored_ref, gain_ref, routes_ref, out_ref, *, experts):
    normed, _ = normalized(stored_ref[...], gain_ref[...])
    (w0, h0, _), (w1, h1, _) = places(routes_ref[...], experts)
    lanes = iota((normed.shape[0], experts * LOW), 1)
    ones = (1.0, 1.0)
    pack(
        normed,
        table(lanes, (w0, w1), ones),
        table(lanes, (h0, h1), ones),
        table(lanes, (h0 + HIGH, h1 + HIGH), ones),
        out_ref,
        0,
    )


def weights_of(normed, router_mat, found):
    logits = mm(normed, router_mat)
    sig = [
        jax.nn.sigmoid(jnp.sum(jnp.where(match, logits, 0.0), axis=1, keepdims=True))
        for _, _, match in found
    ]
    total = sig[0] + sig[1]
    return [s / total for s in sig], sig


def split(value):
    high = value.astype(BF16)
    return high, (value - high.astype(F32)).astype(BF16)


def pack_both(
    stored_ref, cotangent_ref, arrived_ref, gain_ref, router_ref, routes_b_ref, routes_f_ref,
    out_ref, tables_ref, scalars_ref, *, experts,
):
    gain_row = gain_ref[...]
    router_mat = router_ref[...]
    rows, width = stored_ref.shape
    lanes = iota((rows, experts * LOW), 1)
    span = experts * LOW
    saved = 0

    def save(value):
        nonlocal saved
        tables_ref[:, saved * span : (saved + 1) * span] = value.astype(BF16)
        saved += 1

    normed_b, inverse_b = normalized(stored_ref[...], gain_row)
    found_b = places(routes_b_ref[...], experts)
    weights_b, sig_b = weights_of(normed_b, router_mat, found_b)
    scales = [w.astype(BF16).astype(F32) for w in weights_b]
    (w0, h0, _), (w1, h1, _) = found_b
    pack(
        cotangent_ref[...],
        table(lanes, (w0, w1), scales),
        table(lanes, (h0, h1), scales),
        table(lanes, (h0 + HIGH, h1 + HIGH), scales),
        out_ref,
        0,
    )
    ones = (1.0, 1.0)
    save(table(lanes, (w0, w1), ones))
    save(table(lanes, (h0, h1), ones))
    save(table(lanes, (h0 + HIGH, h1 + HIGH), ones))
    for spot in (w0, w1, h0, h1):
        save(jnp.where(lanes == spot, 1.0, 0.0))

    normed_f, _ = normalized(arrived_ref[...], gain_row)
    found_f = places(routes_f_ref[...], experts)
    weights_f, _ = weights_of(normed_f, router_mat, found_f)
    (w0, h0, _), (w1, h1, _) = found_f
    spots = ((w0, w1), (h0, h1), (h0 + HIGH, h1 + HIGH))
    pack(normed_f, *(table(lanes, s, ones) for s in spots), out_ref, width + width // 2)
    for s in spots:
        for part in split(table(lanes, s, weights_f)):
            save(part)
    ratio = [jnp.where(s > 0.0, w / s, 1.0) for w, s in zip(weights_b, scales)]
    kept = [inverse_b, weights_b[0], weights_b[1], sig_b[0], sig_b[1], ratio[0], ratio[1]]
    at = iota((rows, 128), 1)
    scalars = jnp.zeros((rows, 128), F32)
    for i, value in enumerate(kept):
        scalars = jnp.where(at == i, value, scalars)
    scalars_ref[...] = scalars


def half_rows(part, count):
    i = iota((count * HIGH, count * LOW), 0)
    j = iota((count * HIGH, count * LOW), 1)
    left = 2 * i - (i & (HIGH - 1))
    take_left = (j == left).astype(F32).astype(BF16)
    take_right = (j == left + HIGH).astype(F32).astype(BF16)
    return mm(take_left, part).astype(BF16), mm(take_right, part).astype(BF16)


def half_tables(count):
    i = iota((count * LOW, count * HIGH), 1)
    j = iota((count * LOW, count * HIGH), 0)
    left = 2 * i - (i & (HIGH - 1))
    put_left = (j == left).astype(F32).astype(BF16)
    put_right = (j == left + HIGH).astype(F32).astype(BF16)
    return put_left, put_right


def spread(rows_ref, block, sources):
    low = sources * LOW
    width = rows_ref.shape[1]
    half = width // 2
    rows_ref[:low, :] = block[:, :width]
    left, right = half_rows(block[:, width:], sources)
    rows_ref[low:, :half] = left
    rows_ref[low:, half:] = right


def expert_stored(block_ref, gate_ref, up_ref, silu_ref, slope_ref, hidden_ref, rows_ref, *, sources):
    spread(rows_ref, block_ref[...], sources)
    rows = rows_ref[...]
    for f in range(0, gate_ref.shape[1], 256):
        gate = mm(rows, gate_ref[:, f : f + 256])
        up = mm(rows, up_ref[:, f : f + 256])
        sig = jax.nn.sigmoid(gate)
        silu = gate * sig
        silu_ref[:, f : f + 256] = silu
        slope_ref[:, f : f + 256] = up * sig * (1.0 + gate * (1.0 - sig))
        hidden_ref[:, f : f + 256] = (silu * up).astype(BF16)


def expert_both(
    block_ref, silu_ref, slope_ref, hidden_ref, gate_ref, up_ref, down_ref,
    out_ref, rows_ref, grad_gate_ref, grad_up_ref, made_ref, *, sources,
):
    low = sources * LOW
    width = rows_ref.shape[1]
    half = width // 2
    span = width + half
    inner = gate_ref.shape[1]
    put_left, put_right = half_tables(sources)

    def give(at, base):
        both = mm(put_left, made_ref[:, :half]) + mm(put_right, made_ref[:, half:])
        out_ref[:, at + width : at + span] = both.astype(BF16)

    block = block_ref[:, :span]
    spread(rows_ref, block, sources)
    rows = rows_ref[...]
    scores = jnp.zeros((rows.shape[0], 1), F32)
    for f in range(0, inner, 256):
        grad_hidden = mm_nt(rows, down_ref[f : f + 256, :])
        scores += jnp.sum(grad_hidden * hidden_ref[:, f : f + 256].astype(F32), axis=1, keepdims=True)
        grad_up_ref[:, f : f + 256] = (grad_hidden * silu_ref[:, f : f + 256]).astype(BF16)
        grad_gate_ref[:, f : f + 256] = (grad_hidden * slope_ref[:, f : f + 256]).astype(BF16)
    grad_gate = grad_gate_ref[...]
    grad_up = grad_up_ref[...]
    for n in range(0, width, 512):
        made = mm_nt(grad_gate, gate_ref[n : n + 512, :]) + mm_nt(grad_up, up_ref[n : n + 512, :])
        made = made.astype(BF16)
        out_ref[:, n : n + 512] = made[:low]
        made_ref[:, n : n + 512] = made[low:]
    give(0, 0)
    at = iota((low, 128), 1)
    high, rest = split(scores)
    zero = jnp.zeros((low, 128), F32)
    tail = jnp.where(at == 0, high[:low].astype(F32), jnp.where(at == 1, rest[:low].astype(F32), zero))
    at = iota((low // 2, 128), 1)
    zero = jnp.zeros((low // 2, 128), F32)
    more = jnp.where(at == 2, high[low:].astype(F32), jnp.where(at == 3, rest[low:].astype(F32), zero))
    tail = tail + mm(put_left, more.astype(BF16))
    out_ref[:, 2 * span : 2 * span + 128] = tail.astype(BF16)

    spread(rows_ref, block_ref[:, span:], sources)
    rows = rows_ref[...]
    for f in range(0, inner, 256):
        gate = mm(rows, gate_ref[:, f : f + 256])
        up = mm(rows, up_ref[:, f : f + 256])
        grad_up_ref[:, f : f + 256] = (gate * jax.nn.sigmoid(gate) * up).astype(BF16)
    hidden = grad_up_ref[...]
    for n in range(0, width, 512):
        made = mm(hidden, down_ref[:, n : n + 512]).astype(BF16)
        out_ref[:, span + n : span + n + 512] = made[:low]
        made_ref[:, n : n + 512] = made[low:]
    give(span, 0)


def combine(
    back_ref, tables_ref, scalars_ref, arrived_ref, stored_ref, cotangent_ref, gain_ref, router_ref, routes_ref,
    layer_ref, grad_ref, *, experts,
):
    rows, width = arrived_ref.shape
    half = width // 2
    span = width + half
    slots = experts * LOW

    def t(i):
        return tables_ref[:, i * slots : (i + 1) * slots]

    for s, side in ((0, 9), (1, 11)):
        cols = slice(s * half, (s + 1) * half)
        low = back_ref[:, span + s * half : span + (s + 1) * half]
        high = back_ref[:, span + width : 2 * span]
        mixed = mm(t(7), low) + mm(t(8), low) + mm(t(side), high) + mm(t(side + 1), high)
        layer_ref[:, cols] = (arrived_ref[:, cols].astype(F32) + mixed).astype(BF16)

    inverse, w0, w1, s0, s1, r0, r1 = (scalars_ref[:, i : i + 1] for i in range(7))
    extra = back_ref[:, 2 * span : 2 * span + 128]
    u = []
    for k, ratio in ((0, r0), (1, r1)):
        got = mm(t(3 + k), extra)
        more = mm(t(5 + k), extra)
        u.append((got[:, 0:1] + got[:, 1:2] + more[:, 2:3] + more[:, 3:4]) * ratio)
    cross = u[0] * w1 - w0 * u[1]
    columns = iota((rows, experts), 1)
    picks = jnp.where(routes_ref[:, 0:1] == columns, cross * (1.0 - s0), 0.0)
    picks = picks - jnp.where(routes_ref[:, 1:2] == columns, cross * (1.0 - s1), 0.0)
    p0, p1 = split(picks)
    p2 = (picks - p0.astype(F32) - p1.astype(F32)).astype(BF16)

    total = jnp.zeros((rows, 1), F32)
    scaled = []
    for s in range(2):
        cols = slice(s * half, (s + 1) * half)
        high = back_ref[:, width : span]
        grad = mm(t(0), back_ref[:, cols]) + mm(t(1 + s), high)
        router_cols = router_ref[cols, :]
        grad = grad + mm_nt(p0, router_cols) + mm_nt(p1, router_cols) + mm_nt(p2, router_cols)
        grad = grad * gain_ref[:, cols].astype(F32)
        total += jnp.sum(grad * stored_ref[:, cols].astype(F32), axis=1, keepdims=True)
        scaled.append(grad)
    pull = inverse * inverse * inverse * (total / width)
    for s in range(2):
        cols = slice(s * half, (s + 1) * half)
        value = cotangent_ref[:, cols].astype(F32) + inverse * scaled[s]
        grad_ref[:, cols] = (value - stored_ref[:, cols].astype(F32) * pull).astype(BF16)


def call(kernel, outs, scratch=(), limit=48, flops=0, moved=0):
    return pl.pallas_call(
        kernel,
        out_shape=outs,
        scratch_shapes=list(scratch),
        compiler_params=pltpu.CompilerParams(vmem_limit_bytes=limit * 2**20),
        cost_estimate=pl.CostEstimate(flops=flops, bytes_accessed=moved, transcendentals=0),
    )


def body(
    activations, gradients, stashed, norm_gain, router, gate_weight, up_weight, down_weight, routes_forward, routes_backward
):
    shape = jax.ShapeDtypeStruct
    experts = lax.axis_size("expert")
    rows, width = stashed.shape[1:]
    span = width + width // 2
    inner = gate_weight.shape[3]
    low, slots = experts * LOW, experts * (LOW + HIGH)
    gate_mat, up_mat, down_mat = gate_weight[0, 0], up_weight[0, 0], down_weight[0, 0]
    router_mat, stored = router[0], stashed[0]
    routes_f, routes_b = routes_forward[0], routes_backward[0]

    def exchange(block):
        blocks = block.reshape(experts, LOW, block.shape[1])
        return lax.all_to_all(blocks, "expert", split_axis=0, concat_axis=0, tiled=True).reshape(block.shape)

    arrived = passed_along(activations, "section", 1)[0]
    cotangent = passed_along(gradients, "section", -1)[0]

    sent_b = call(
        functools.partial(pack_stored, experts=experts), shape((low, span), BF16), flops=4 * low * rows * width, moved=2**22
    )(stored, norm_gain, routes_b)
    got_b = exchange(sent_b)
    sent, tables, scalars = call(
        functools.partial(pack_both, experts=experts),
        (shape((low, 2 * span), BF16), shape((rows, 13 * low), BF16), shape((rows, 128), F32)),
        flops=10 * low * rows * width,
        moved=2**23,
    )(stored, cotangent, arrived, norm_gain, router_mat, routes_b, routes_f)
    got = exchange(sent)
    silu, slope, hidden = call(
        functools.partial(expert_stored, sources=experts),
        (shape((slots, inner), F32), shape((slots, inner), F32), shape((slots, inner), BF16)),
        scratch=[pltpu.VMEM((slots, width), BF16)],
        flops=4 * slots * width * inner,
        moved=2**24,
    )(got_b, gate_mat, up_mat)
    made = call(
        functools.partial(expert_both, sources=experts),
        shape((low, 2 * span + 128), BF16),
        scratch=[
            pltpu.VMEM((slots, width), BF16),
            pltpu.VMEM((slots, inner), BF16),
            pltpu.VMEM((slots, inner), BF16),
            pltpu.VMEM((slots - low, width), BF16),
        ],
        flops=12 * slots * width * inner,
        moved=2**24,
    )(got, silu, slope, hidden, gate_mat, up_mat, down_mat)
    back = exchange(made)
    layer_out, input_grad = call(
        functools.partial(combine, experts=experts),
        (shape((rows, width), BF16), shape((rows, width), BF16)),
        flops=20 * low * rows * width,
        moved=2**23,
    )(back, tables, scalars, arrived, stored, cotangent, norm_gain, router_mat, routes_b)
    return layer_out[None], input_grad[None]


def solution(mesh):
    spread_rows = P("section", "expert", None)
    weights = P("section", "expert", None, None)
    placed = (
        spread_rows,
        spread_rows,
        spread_rows,
        P("section", None),
        P("section", None, None),
        weights,
        weights,
        weights,
        spread_rows,
        spread_rows,
    )
    return jax.shard_map(body, mesh=mesh, in_specs=placed, out_specs=(spread_rows, spread_rows), check_vma=False)
```

```python
import functools

import jax
import jax.numpy as jnp
from jax import lax
from jax.experimental import pallas as pl
from jax.experimental.pallas import tpu as pltpu
from jax.sharding import PartitionSpec as P


NORM_EPS = 1e-06
LOW = 8
HIGH = 4
F32 = jnp.float32
BF16 = jnp.bfloat16
NT = (((1,), (1,)), ((), ()))
ANY = pl.BlockSpec(memory_space=pl.ANY)
HBM = pl.BlockSpec(memory_space=pltpu.HBM)
VMEM = pl.BlockSpec(memory_space=pltpu.VMEM)


def passed_along(value, axis, steps):
    count = lax.axis_size(axis)
    pairs = [(source, (source + steps) % count) for source in range(count)]
    return lax.ppermute(value, axis, pairs)


def mm(a, b):
    return jnp.dot(a, b, preferred_element_type=F32)


def mm_nt(a, b):
    return lax.dot_general(a, b, NT, preferred_element_type=F32)


def iota(shape, dim):
    return lax.broadcasted_iota(jnp.int32, shape, dim)


def mask(condition):
    return condition.astype(F32).astype(BF16)


class Copies:
    def __init__(self, sems):
        self.sems = sems
        self.used = 0

    def start(self, source, target):
        copy = pltpu.make_async_copy(source, target, self.sems.at[self.used])
        self.used += 1
        copy.start()
        return copy


def normalized(tokens, gain_row):
    values = tokens.astype(F32)
    inverse = lax.rsqrt(jnp.mean(values * values, axis=-1, keepdims=True) + NORM_EPS)
    return (values * inverse * gain_row.astype(F32)).astype(BF16), inverse


def places(routes, experts):
    count = routes.shape[1]
    experts_at = iota((experts, count), 0)
    matches = [routes[k : k + 1, :] == experts_at for k in range(2)]
    named = mask(matches[0] | matches[1])
    earlier = mm(named, mask(iota((count, count), 0) < iota((count, count), 1)))
    found = []
    for k in range(2):
        slot = jnp.sum(jnp.where(matches[k], earlier, 0.0), axis=0, keepdims=True).astype(jnp.int32)
        base = routes[k : k + 1, :] * LOW
        whole = jnp.where(slot < LOW, base + slot, -LOW)
        half = jnp.where(slot < LOW, -LOW, base + slot - LOW)
        found.append((whole, half, matches[k]))
    return found


def spots_of(found):
    (w0, h0, _), (w1, h1, _) = found
    return (w0, w1), (h0, h1), (h0 + HIGH, h1 + HIGH)


def table(at, spots, scales=(1.0, 1.0)):
    total = jnp.where(at == spots[0], scales[0], 0.0)
    return total + jnp.where(at == spots[1], scales[1], 0.0)


def pack(tokens, tables, made_ref, out_ref, at, copies):
    whole, left, right = (t.astype(BF16) for t in tables)
    half = tokens.shape[1] // 2
    running = []

    def give(value, column):
        cols = slice(at + column, at + column + half)
        made_ref[:, cols] = value.astype(BF16)
        running.append(copies.start(made_ref.at[:, cols], out_ref.at[:, cols]))

    give(mm(whole, tokens[:, :half]), 0)
    give(mm(whole, tokens[:, half:]), half)
    give(mm(left, tokens[:, :half]) + mm(right, tokens[:, half:]), 2 * half)
    return running


def pack_stored(stored_ref, gain_ref, routes_ref, out_ref, made_ref, sems, *, experts):
    found = places(routes_ref[...], experts)
    at = iota((experts * LOW, routes_ref.shape[1]), 0)
    normed, _ = normalized(stored_ref[...], gain_ref[...])
    for copy in pack(normed, [table(at, s) for s in spots_of(found)], made_ref, out_ref, 0, Copies(sems)):
        copy.wait()


def weights_of(normed, router_rows, found):
    logits = mm_nt(router_rows, normed)
    sig = [
        jax.nn.sigmoid(jnp.sum(jnp.where(match, logits, 0.0), axis=0, keepdims=True))
        for _, _, match in found
    ]
    total = sig[0] + sig[1]
    return [s / total for s in sig], sig


def split(value):
    high = value.astype(BF16)
    return high, (value - high.astype(F32)).astype(BF16)


def pack_both(
    stored_ref, cotangent_ref, arrived_ref, gain_ref, router_ref, routes_b_ref, routes_f_ref,
    out_ref, tables_ref, scalars_ref, made_ref, sems, *, experts,
):
    gain_row = gain_ref[...]
    router_rows = router_ref[...]
    rows, width = stored_ref.shape
    span = experts * LOW
    at = iota((span, rows), 0)
    copies = Copies(sems)

    normed_b, inverse_b = normalized(stored_ref[...], gain_row)
    found_b = places(routes_b_ref[...], experts)
    weights_b, sig_b = weights_of(normed_b, router_rows, found_b)
    scales = [w.astype(BF16).astype(F32) for w in weights_b]
    spots_b = spots_of(found_b)
    running = pack(cotangent_ref[...], [table(at, s, scales) for s in spots_b], made_ref, out_ref, 0, copies)
    normed_f, _ = normalized(arrived_ref[...], gain_row)
    found_f = places(routes_f_ref[...], experts)
    spots_f = spots_of(found_f)
    running += pack(normed_f, [table(at, s) for s in spots_f], made_ref, out_ref, width + width // 2, copies)
    weights_f, _ = weights_of(normed_f, router_rows, found_f)

    kept = [table(at, s) for s in spots_b]
    kept += [jnp.where(at == s, 1.0, 0.0) for s in (*spots_b[0], *spots_b[1])]
    for s in spots_f:
        kept += [part.astype(F32) for part in split(table(at, s, weights_f))]
    for i, value in enumerate(kept):
        tables_ref[:, i * span : (i + 1) * span] = value.T.astype(BF16)

    ratio = [jnp.where(s > 0.0, w / s, 1.0) for w, s in zip(weights_b, scales)]
    routes_b = routes_b_ref[...].astype(F32)
    lines = [*weights_b, *sig_b, *ratio, routes_b[0:1], routes_b[1:2]]
    line_at = iota((rows, rows), 0)
    scalars = jnp.zeros((rows, rows), F32)
    for i, value in enumerate(lines):
        scalars = jnp.where(line_at == i, value, scalars)
    scalars_ref[...] = jnp.where(iota((rows, rows), 1) == len(lines), inverse_b, scalars.T)
    for copy in running:
        copy.wait()


def half_places(count):
    i = iota((count * HIGH, count * LOW), 0)
    j = iota((count * HIGH, count * LOW), 1)
    left = 2 * i - (i & (HIGH - 1))
    return mask(j == left), mask(j == left + HIGH)


def half_homes(count):
    i = iota((count * LOW, count * HIGH), 1)
    j = iota((count * LOW, count * HIGH), 0)
    left = 2 * i - (i & (HIGH - 1))
    return mask(j == left), mask(j == left + HIGH)


def join_halves(rows_ref, part, sources):
    low = sources * LOW
    half = rows_ref.shape[1] // 2
    take_left, take_right = half_places(sources)
    rows_ref[low:, :half] = mm(take_left, part).astype(BF16)
    rows_ref[low:, half:] = mm(take_right, part).astype(BF16)


def expert_stored(block_ref, gate_ref, up_ref, kept_ref, rows_ref, *, sources):
    low = sources * LOW
    width = rows_ref.shape[1]
    rows_ref[:low, :] = block_ref[:, :width]
    join_halves(rows_ref, block_ref[:, width:], sources)
    rows = rows_ref[...]
    for f in range(0, gate_ref.shape[1], 256):
        gate = mm(rows, gate_ref[:, f : f + 256])
        up = mm(rows, up_ref[:, f : f + 256])
        sig = jax.nn.sigmoid(gate)
        silu = gate * sig
        kept_ref[:, f * 3 : f * 3 + 256] = silu
        kept_ref[:, f * 3 + 256 : f * 3 + 512] = up * sig * (1.0 + gate * (1.0 - sig))
        kept_ref[:, f * 3 + 512 : f * 3 + 768] = (silu * up).astype(BF16).astype(F32)


def expert_both(
    block_any, kept_any, gate_any, up_any, down_any, out_any,
    rows_b, half_b, rows_f, half_f, kept_ref, gate_ref, up_ref, down_ref, grad_gate_ref, grad_up_ref, made_ref, out_ref, sems, *, sources,
):
    low = sources * LOW
    width = rows_b.shape[1]
    half = width // 2
    span = width + half
    inner = gate_ref.shape[1]
    step = 256
    wide = 512
    copies = Copies(sems)
    part_b = copies.start(block_any.at[:, width:span], half_b)
    low_b = copies.start(block_any.at[:, :width], rows_b.at[:low, :])
    downs = []
    helds = []
    for f in range(0, inner, step):
        downs.append(copies.start(down_any.at[f : f + step, :], down_ref.at[f : f + step, :]))
        cols = slice(3 * f, 3 * f + 3 * step)
        helds.append(copies.start(kept_any.at[:, cols], kept_ref.at[:, cols]))
    put_left, put_right = half_homes(sources)
    part_b.wait()
    join_halves(rows_b, half_b[...], sources)
    low_b.wait()
    gates = []
    ups = []

    rows = rows_b[...]
    scores = jnp.zeros((rows.shape[0], 1), F32)
    for i, f in enumerate(range(0, inner, step)):
        downs[i].wait()
        grad_hidden = mm_nt(rows, down_ref[f : f + step, :])
        helds[i].wait()
        if i == len(range(0, inner, step)) - 1:
            for n in range(0, width, wide):
                gates.append(copies.start(gate_any.at[n : n + wide, :], gate_ref.at[n : n + wide, :]))
                ups.append(copies.start(up_any.at[n : n + wide, :], up_ref.at[n : n + wide, :]))
            part_f = copies.start(block_any.at[:, span + width :], half_f)
            low_f = copies.start(block_any.at[:, span : span + width], rows_f.at[:low, :])
        cols = slice(f, f + step)
        silu, slope, hidden = (kept_ref[:, 3 * f + j * step : 3 * f + (j + 1) * step] for j in range(3))
        scores += jnp.sum(grad_hidden * hidden, axis=1, keepdims=True)
        grad_up_ref[:, cols] = (grad_hidden * silu).astype(BF16)
        grad_gate_ref[:, cols] = (grad_hidden * slope).astype(BF16)

    at = iota((low, 128), 1)
    high, rest = split(scores)
    tail = jnp.where(at == 0, high[:low].astype(F32), jnp.where(at == 1, rest[:low].astype(F32), 0.0))
    at = iota((low // 2, 128), 1)
    more = jnp.where(at == 2, high[low:].astype(F32), jnp.where(at == 3, rest[low:].astype(F32), 0.0))
    out_ref[:, 2 * span :] = (tail + mm(put_left, more.astype(BF16))).astype(BF16)
    given = [copies.start(out_ref.at[:, 2 * span :], out_any.at[:, 2 * span :])]

    def give(columns):
        given.append(copies.start(out_ref.at[:, columns], out_any.at[:, columns]))

    def give_halves(base):
        both = mm(put_left, made_ref[:, :half]) + mm(put_right, made_ref[:, half:])
        out_ref[:, base + width : base + span] = both.astype(BF16)
        give(slice(base + width, base + span))

    grad_gate = grad_gate_ref[...]
    grad_up = grad_up_ref[...]
    for i, n in enumerate(range(0, width, wide)):
        gates[i].wait()
        ups[i].wait()
        cols = slice(n, n + wide)
        made = (mm_nt(grad_gate, gate_ref[cols, :]) + mm_nt(grad_up, up_ref[cols, :])).astype(BF16)
        out_ref[:, cols] = made[:low]
        made_ref[:, cols] = made[low:]
        give(cols)
    give_halves(0)

    part_f.wait()
    join_halves(rows_f, half_f[...], sources)
    low_f.wait()
    rows = rows_f[...]
    for f in range(0, inner, step):
        gate = mm(rows, gate_ref[:, f : f + step])
        up = mm(rows, up_ref[:, f : f + step])
        grad_up_ref[:, f : f + step] = (gate * jax.nn.sigmoid(gate) * up).astype(BF16)
    hidden = grad_up_ref[...]
    for n in range(0, width, wide):
        made = mm(hidden, down_ref[:, n : n + wide]).astype(BF16)
        cols = slice(span + n, span + n + wide)
        out_ref[:, cols] = made[:low]
        made_ref[:, n : n + wide] = made[low:]
        give(cols)
    give_halves(span)
    for copy in given:
        copy.wait()


def combine(
    back_any, tables_any, scalars_ref, arrived_any, stored_any, cotangent_any, gain_ref, router_ref, layer_any, grad_any,
    back_ref, tables_ref, arrived_ref, stored_ref, cotangent_ref, layer_ref, grad_ref, sems, *, experts,
):
    rows, width = arrived_ref.shape
    half = width // 2
    span = width + half
    slots = experts * LOW
    copies = Copies(sems)

    def columns(source, target, cols):
        return copies.start(source.at[:, cols], target.at[:, cols])

    first = [
        columns(back_any, back_ref, slice(2 * span, 2 * span + 128)),
        columns(tables_any, tables_ref, slice(0, 7 * slots)),
        columns(back_any, back_ref, slice(0, span)),
        copies.start(stored_any, stored_ref),
    ]
    second = [
        columns(tables_any, tables_ref, slice(7 * slots, 13 * slots)),
        columns(back_any, back_ref, slice(span, 2 * span)),
        copies.start(arrived_any, arrived_ref),
        copies.start(cotangent_any, cotangent_ref),
    ]

    def t(i):
        return tables_ref[:, i * slots : (i + 1) * slots]

    w0, w1, s0, s1, r0, r1, e0, e1, inverse = (scalars_ref[:, i : i + 1] for i in range(9))
    first[0].wait()
    first[1].wait()
    extra = back_ref[:, 2 * span : 2 * span + 128]
    u = []
    for k, ratio in ((0, r0), (1, r1)):
        got = mm(t(3 + k), extra)
        more = mm(t(5 + k), extra)
        u.append((got[:, 0:1] + got[:, 1:2] + more[:, 2:3] + more[:, 3:4]) * ratio)
    cross = u[0] * w1 - w0 * u[1]
    expert_at = iota((rows, experts), 1).astype(F32)
    picks = jnp.where(e0 == expert_at, cross * (1.0 - s0), 0.0)
    picks = picks - jnp.where(e1 == expert_at, cross * (1.0 - s1), 0.0)
    p0, p1 = split(picks)
    p2 = (picks - p0.astype(F32) - p1.astype(F32)).astype(BF16)
    first[2].wait()
    first[3].wait()
    total = jnp.zeros((rows, 1), F32)
    scaled = []
    high = back_ref[:, width:span]
    for s in range(2):
        cols = slice(s * half, (s + 1) * half)
        grad = mm(t(0), back_ref[:, cols]) + mm(t(1 + s), high)
        router_cols = router_ref[:, cols]
        grad = grad + mm(p0, router_cols) + mm(p1, router_cols) + mm(p2, router_cols)
        grad = grad * gain_ref[:, cols].astype(F32)
        total += jnp.sum(grad * stored_ref[:, cols].astype(F32), axis=1, keepdims=True)
        scaled.append(grad)
    pull = inverse * inverse * inverse * (total / width)
    for copy in second:
        copy.wait()
    given = []
    for s in range(2):
        cols = slice(s * half, (s + 1) * half)
        value = cotangent_ref[:, cols].astype(F32) + inverse * scaled[s]
        grad_ref[:, cols] = (value - stored_ref[:, cols].astype(F32) * pull).astype(BF16)
        given.append(columns(grad_ref, grad_any, cols))
    high = back_ref[:, span + width : 2 * span]
    for s, side in ((0, 9), (1, 11)):
        cols = slice(s * half, (s + 1) * half)
        low = back_ref[:, span + s * half : span + (s + 1) * half]
        mixed = mm(t(7), low) + mm(t(8), low) + mm(t(side), high) + mm(t(side + 1), high)
        layer_ref[:, cols] = (arrived_ref[:, cols].astype(F32) + mixed).astype(BF16)
        given.append(columns(layer_ref, layer_any, cols))
    for copy in given:
        copy.wait()


def call(kernel, ins, outs, out_specs, scratch=(), sems=0, flops=0, moved=0, limit=60):
    return pl.pallas_call(
        kernel,
        in_specs=ins,
        out_specs=out_specs,
        out_shape=outs,
        scratch_shapes=list(scratch) + ([pltpu.SemaphoreType.DMA((sems,))] if sems else []),
        compiler_params=pltpu.CompilerParams(vmem_limit_bytes=limit * 2**20),
        cost_estimate=pl.CostEstimate(flops=flops, bytes_accessed=moved, transcendentals=0),
    )


def body(
    activations, gradients, stashed, norm_gain, router, gate_weight, up_weight, down_weight, routes_forward, routes_backward
):
    shape = jax.ShapeDtypeStruct
    experts = lax.axis_size("expert")
    rows, width = stashed.shape[1:]
    span = width + width // 2
    inner = gate_weight.shape[3]
    low, slots = experts * LOW, experts * (LOW + HIGH)
    gate_mat, up_mat, down_mat = gate_weight[0, 0], up_weight[0, 0], down_weight[0, 0]
    router_rows, stored = router[0].T, stashed[0]
    routes_f, routes_b = routes_forward[0].T, routes_backward[0].T

    def exchange(block):
        blocks = block.reshape(experts, LOW, block.shape[1])
        return lax.all_to_all(blocks, "expert", split_axis=0, concat_axis=0, tiled=True).reshape(block.shape)

    arrived = passed_along(activations, "section", 1)[0]
    cotangent = passed_along(gradients, "section", -1)[0]

    sent_b = call(
        functools.partial(pack_stored, experts=experts),
        [VMEM] * 3,
        shape((low, span), BF16),
        HBM,
        scratch=[pltpu.VMEM((low, span), BF16)],
        sems=3,
        flops=4 * low * rows * width,
        moved=2**22,
    )(stored, norm_gain, routes_b)
    got_b = exchange(sent_b)
    sent, tables, scalars = call(
        functools.partial(pack_both, experts=experts),
        [VMEM] * 7,
        (shape((low, 2 * span), BF16), shape((rows, 13 * low), BF16), shape((rows, rows), F32)),
        (HBM, VMEM, VMEM),
        scratch=[pltpu.VMEM((low, 2 * span), BF16)],
        sems=6,
        flops=10 * low * rows * width,
        moved=2**23,
    )(stored, cotangent, arrived, norm_gain, router_rows, routes_b, routes_f)
    got = exchange(sent)
    kept = call(
        functools.partial(expert_stored, sources=experts),
        [VMEM] * 3,
        shape((slots, 3 * inner), F32),
        VMEM,
        scratch=[pltpu.VMEM((slots, width), BF16)],
        limit=40,
        flops=4 * slots * width * inner,
        moved=2**24,
    )(got_b, gate_mat, up_mat)
    made = call(
        functools.partial(expert_both, sources=experts),
        [HBM] * 5,
        shape((low, 2 * span + 128), BF16),
        HBM,
        scratch=[
            pltpu.VMEM((slots, width), BF16),
            pltpu.VMEM((low, width // 2), BF16),
            pltpu.VMEM((slots, width), BF16),
            pltpu.VMEM((low, width // 2), BF16),
            pltpu.VMEM((slots, 3 * inner), F32),
            pltpu.VMEM((width, inner), BF16),
            pltpu.VMEM((width, inner), BF16),
            pltpu.VMEM((inner, width), BF16),
            pltpu.VMEM((slots, inner), BF16),
            pltpu.VMEM((slots, inner), BF16),
            pltpu.VMEM((slots - low, width), BF16),
            pltpu.VMEM((low, 2 * span + 128), BF16),
        ],
        sems=40,
        limit=58,
        flops=12 * slots * width * inner,
        moved=2**24,
    )(got, kept, gate_mat, up_mat, down_mat)
    back = exchange(made)
    layer_out, input_grad = call(
        functools.partial(combine, experts=experts),
        [ANY, HBM, VMEM, HBM, HBM, HBM, VMEM, VMEM],
        (shape((rows, width), BF16), shape((rows, width), BF16)),
        (HBM, HBM),
        scratch=[
            pltpu.VMEM((low, 2 * span + 128), BF16),
            pltpu.VMEM((rows, 13 * low), BF16),
            *[pltpu.VMEM((rows, width), BF16)] * 5,
        ],
        sems=12,
        flops=20 * low * rows * width,
        moved=2**23,
    )(back, tables, scalars, arrived, stored, cotangent, norm_gain, router_rows)
    return layer_out[None], input_grad[None]


def solution(mesh):
    spread_rows = P("section", "expert", None)
    weights = P("section", "expert", None, None)
    placed = (
        spread_rows,
        spread_rows,
        spread_rows,
        P("section", None),
        P("section", None, None),
        weights,
        weights,
        weights,
        spread_rows,
        spread_rows,
    )
    return jax.shard_map(body, mesh=mesh, in_specs=placed, out_specs=(spread_rows, spread_rows), check_vma=False)
```

```python
import functools

import jax
import jax.numpy as jnp
from jax import lax
from jax.experimental import pallas as pl
from jax.experimental.pallas import tpu as pltpu
from jax.sharding import PartitionSpec as P


NORM_EPS = 1e-06
LOW = 8
HIGH = 4
F32 = jnp.float32
BF16 = jnp.bfloat16
NT = (((1,), (1,)), ((), ()))
ANY = pl.BlockSpec(memory_space=pl.ANY)
HBM = pl.BlockSpec(memory_space=pltpu.HBM)
VMEM = pl.BlockSpec(memory_space=pltpu.VMEM)


def passed_along(value, axis, steps):
    count = lax.axis_size(axis)
    pairs = [(source, (source + steps) % count) for source in range(count)]
    return lax.ppermute(value, axis, pairs)


def mm(a, b):
    return jnp.dot(a, b, preferred_element_type=F32)


def mm_nt(a, b):
    return lax.dot_general(a, b, NT, preferred_element_type=F32)


def iota(shape, dim):
    return lax.broadcasted_iota(jnp.int32, shape, dim)


def mask(condition):
    return condition.astype(F32).astype(BF16)


class Copies:
    def __init__(self, sems):
        self.sems = sems
        self.used = 0

    def start(self, source, target):
        copy = pltpu.make_async_copy(source, target, self.sems.at[self.used])
        self.used += 1
        copy.start()
        return copy


def normalized(tokens, gain_row):
    values = tokens.astype(F32)
    inverse = lax.rsqrt(jnp.mean(values * values, axis=-1, keepdims=True) + NORM_EPS)
    return (values * inverse * gain_row.astype(F32)).astype(BF16), inverse


def places(routes, experts):
    count = routes.shape[1]
    experts_at = iota((experts, count), 0)
    matches = [routes[k : k + 1, :] == experts_at for k in range(2)]
    named = mask(matches[0] | matches[1])
    earlier = mm(named, mask(iota((count, count), 0) < iota((count, count), 1)))
    found = []
    for k in range(2):
        slot = jnp.sum(jnp.where(matches[k], earlier, 0.0), axis=0, keepdims=True).astype(jnp.int32)
        base = routes[k : k + 1, :] * LOW
        whole = jnp.where(slot < LOW, base + slot, -LOW)
        half = jnp.where(slot < LOW, -LOW, base + slot - LOW)
        found.append((whole, half, matches[k]))
    return found


def spots_of(found):
    (w0, h0, _), (w1, h1, _) = found
    return (w0, w1), (h0, h1), (h0 + HIGH, h1 + HIGH)


def table(at, spots, scales=(1.0, 1.0)):
    total = jnp.where(at == spots[0], scales[0], 0.0)
    return total + jnp.where(at == spots[1], scales[1], 0.0)


def pack(tokens, tables, made_ref, out_ref, at, copies):
    whole, left, right = (t.astype(BF16) for t in tables)
    half = tokens.shape[1] // 2
    running = []

    def give(value, column):
        cols = slice(at + column, at + column + half)
        made_ref[:, cols] = value.astype(BF16)
        running.append(copies.start(made_ref.at[:, cols], out_ref.at[:, cols]))

    give(mm(whole, tokens[:, :half]), 0)
    give(mm(whole, tokens[:, half:]), half)
    give(mm(left, tokens[:, :half]) + mm(right, tokens[:, half:]), 2 * half)
    return running


def pack_stored(stored_ref, gain_ref, routes_ref, out_ref, made_ref, sems, *, experts):
    found = places(routes_ref[...], experts)
    at = iota((experts * LOW, routes_ref.shape[1]), 0)
    normed, _ = normalized(stored_ref[...], gain_ref[...])
    for copy in pack(normed, [table(at, s) for s in spots_of(found)], made_ref, out_ref, 0, Copies(sems)):
        copy.wait()


def weights_of(normed, router_rows, found):
    logits = mm_nt(router_rows, normed)
    sig = [
        jax.nn.sigmoid(jnp.sum(jnp.where(match, logits, 0.0), axis=0, keepdims=True))
        for _, _, match in found
    ]
    total = sig[0] + sig[1]
    return [s / total for s in sig], sig


def split(value):
    high = value.astype(BF16)
    return high, (value - high.astype(F32)).astype(BF16)


def pack_both(
    stored_ref, cotangent_ref, arrived_ref, gain_ref, router_ref, routes_b_ref, routes_f_ref,
    out_ref, tables_ref, scalars_ref, made_ref, sems, *, experts,
):
    gain_row = gain_ref[...]
    router_rows = router_ref[...]
    rows, width = stored_ref.shape
    span = experts * LOW
    at = iota((span, rows), 0)
    copies = Copies(sems)

    normed_b, inverse_b = normalized(stored_ref[...], gain_row)
    found_b = places(routes_b_ref[...], experts)
    weights_b, sig_b = weights_of(normed_b, router_rows, found_b)
    scales = [w.astype(BF16).astype(F32) for w in weights_b]
    spots_b = spots_of(found_b)
    running = pack(cotangent_ref[...], [table(at, s, scales) for s in spots_b], made_ref, out_ref, 0, copies)
    normed_f, _ = normalized(arrived_ref[...], gain_row)
    found_f = places(routes_f_ref[...], experts)
    spots_f = spots_of(found_f)
    running += pack(normed_f, [table(at, s) for s in spots_f], made_ref, out_ref, width + width // 2, copies)
    weights_f, _ = weights_of(normed_f, router_rows, found_f)

    kept = [table(at, s) for s in spots_b]
    kept += [jnp.where(at == s, 1.0, 0.0) for s in (*spots_b[0], *spots_b[1])]
    for s in spots_f:
        kept += [part.astype(F32) for part in split(table(at, s, weights_f))]
    for i, value in enumerate(kept):
        tables_ref[:, i * span : (i + 1) * span] = value.T.astype(BF16)

    ratio = [jnp.where(s > 0.0, w / s, 1.0) for w, s in zip(weights_b, scales)]
    routes_b = routes_b_ref[...].astype(F32)
    lines = [*weights_b, *sig_b, *ratio, routes_b[0:1], routes_b[1:2]]
    line_at = iota((rows, rows), 0)
    scalars = jnp.zeros((rows, rows), F32)
    for i, value in enumerate(lines):
        scalars = jnp.where(line_at == i, value, scalars)
    scalars_ref[...] = jnp.where(iota((rows, rows), 1) == len(lines), inverse_b, scalars.T)
    for copy in running:
        copy.wait()


def half_places(count):
    i = iota((count * HIGH, count * LOW), 0)
    j = iota((count * HIGH, count * LOW), 1)
    left = 2 * i - (i & (HIGH - 1))
    return mask(j == left), mask(j == left + HIGH)


def half_homes(count):
    i = iota((count * LOW, count * HIGH), 1)
    j = iota((count * LOW, count * HIGH), 0)
    left = 2 * i - (i & (HIGH - 1))
    return mask(j == left), mask(j == left + HIGH)


def join_halves(rows_ref, part, sources):
    low = sources * LOW
    half = rows_ref.shape[1] // 2
    take_left, take_right = half_places(sources)
    rows_ref[low:, :half] = mm(take_left, part).astype(BF16)
    rows_ref[low:, half:] = mm(take_right, part).astype(BF16)


def expert_stored(block_ref, gate_ref, up_ref, silu_ref, slope_ref, hidden_ref, rows_ref, *, sources):
    low = sources * LOW
    width = rows_ref.shape[1]
    rows_ref[:low, :] = block_ref[:, :width]
    join_halves(rows_ref, block_ref[:, width:], sources)
    rows = rows_ref[...]
    for f in range(0, gate_ref.shape[1], 256):
        gate = mm(rows, gate_ref[:, f : f + 256])
        up = mm(rows, up_ref[:, f : f + 256])
        sig = jax.nn.sigmoid(gate)
        silu = gate * sig
        silu_ref[:, f : f + 256] = silu
        slope_ref[:, f : f + 256] = up * sig * (1.0 + gate * (1.0 - sig))
        hidden_ref[:, f : f + 256] = (silu * up).astype(BF16)


def expert_both(
    block_any, silu_ref, slope_ref, hidden_ref, gate_any, up_any, down_any, out_any,
    rows_b, half_b, rows_f, half_f, gate_ref, up_ref, down_ref, grad_gate_ref, grad_up_ref, made_ref, out_ref, sems,
    *, sources,
):
    low = sources * LOW
    width = rows_b.shape[1]
    half = width // 2
    span = width + half
    inner = gate_ref.shape[1]
    step = 256
    wide = 512
    copies = Copies(sems)

    def started(source, target, step):
        count = target.shape[0]
        return [copies.start(source.at[i : i + step, :], target.at[i : i + step, :]) for i in range(0, count, step)]

    def taken(running):
        for copy in running:
            copy.wait()

    first = [
        copies.start(block_any.at[:, width:span], half_b),
        copies.start(block_any.at[:, :width], rows_b.at[:low, :]),
        *started(down_any, down_ref, inner // 2),
    ]
    taken(first[:2])
    second = started(gate_any, gate_ref, width // 2)
    join_halves(rows_b, half_b[...], sources)
    taken(first[2:])
    second += started(up_any, up_ref, width // 2)
    scores = jnp.zeros((rows_b.shape[0], 1), F32)
    for f in range(0, inner, step):
        cols = slice(f, f + step)
        grad_hidden = mm_nt(rows_b[...], down_ref[cols, :])
        scores += jnp.sum(grad_hidden * hidden_ref[:, cols].astype(F32), axis=1, keepdims=True)
        grad_up_ref[:, cols] = (grad_hidden * silu_ref[:, cols]).astype(BF16)
        grad_gate_ref[:, cols] = (grad_hidden * slope_ref[:, cols]).astype(BF16)

    put_left, _ = half_homes(sources)
    at = iota((low, 128), 1)
    high, rest = split(scores)
    tail = jnp.where(at == 0, high[:low].astype(F32), jnp.where(at == 1, rest[:low].astype(F32), 0.0))
    at = iota((low // 2, 128), 1)
    more = jnp.where(at == 2, high[low:].astype(F32), jnp.where(at == 3, rest[low:].astype(F32), 0.0))
    out_ref[:, 2 * span :] = (tail + mm(put_left, more.astype(BF16))).astype(BF16)
    given = [copies.start(out_ref.at[:, 2 * span :], out_any.at[:, 2 * span :])]

    def give(columns):
        given.append(copies.start(out_ref.at[:, columns], out_any.at[:, columns]))

    def give_halves(base):
        put_left, put_right = half_homes(sources)
        both = mm(put_left, made_ref[:, :half]) + mm(put_right, made_ref[:, half:])
        out_ref[:, base + width : base + span] = both.astype(BF16)
        give(slice(base + width, base + span))

    taken(second)
    third = [
        copies.start(block_any.at[:, span + width :], half_f),
        copies.start(block_any.at[:, span : span + width], rows_f.at[:low, :]),
    ]
    for n in range(0, width, wide):
        cols = slice(n, n + wide)
        made = (mm_nt(grad_gate_ref[...], gate_ref[cols, :]) + mm_nt(grad_up_ref[...], up_ref[cols, :])).astype(BF16)
        out_ref[:, cols] = made[:low]
        made_ref[:, cols] = made[low:]
        give(cols)
    give_halves(0)

    taken(third)
    join_halves(rows_f, half_f[...], sources)
    for f in range(0, inner, step):
        gate = mm(rows_f[...], gate_ref[:, f : f + step])
        up = mm(rows_f[...], up_ref[:, f : f + step])
        grad_up_ref[:, f : f + step] = (gate * jax.nn.sigmoid(gate) * up).astype(BF16)
    for n in range(0, width, wide):
        made = mm(grad_up_ref[...], down_ref[:, n : n + wide]).astype(BF16)
        cols = slice(span + n, span + n + wide)
        out_ref[:, cols] = made[:low]
        made_ref[:, n : n + wide] = made[low:]
        give(cols)
    give_halves(span)
    for copy in given:
        copy.wait()


def combine(
    back_ref, tables_ref, scalars_ref, arrived_ref, stored_ref, cotangent_ref, gain_ref, router_ref, layer_ref, grad_ref,
    *, experts,
):
    rows, width = arrived_ref.shape
    half = width // 2
    span = width + half
    slots = experts * LOW

    def t(i):
        return tables_ref[:, i * slots : (i + 1) * slots]

    high = back_ref[:, span + width : 2 * span]
    for s, side in ((0, 9), (1, 11)):
        cols = slice(s * half, (s + 1) * half)
        low = back_ref[:, span + s * half : span + (s + 1) * half]
        mixed = mm(t(7), low) + mm(t(8), low) + mm(t(side), high) + mm(t(side + 1), high)
        layer_ref[:, cols] = (arrived_ref[:, cols].astype(F32) + mixed).astype(BF16)

    w0, w1, s0, s1, r0, r1, e0, e1, inverse = (scalars_ref[:, i : i + 1] for i in range(9))
    extra = back_ref[:, 2 * span : 2 * span + 128]
    u = []
    for k, ratio in ((0, r0), (1, r1)):
        got = mm(t(3 + k), extra)
        more = mm(t(5 + k), extra)
        u.append((got[:, 0:1] + got[:, 1:2] + more[:, 2:3] + more[:, 3:4]) * ratio)
    cross = u[0] * w1 - w0 * u[1]
    expert_at = iota((rows, experts), 1).astype(F32)
    picks = jnp.where(e0 == expert_at, cross * (1.0 - s0), 0.0)
    picks = picks - jnp.where(e1 == expert_at, cross * (1.0 - s1), 0.0)
    p0, p1 = split(picks)
    p2 = (picks - p0.astype(F32) - p1.astype(F32)).astype(BF16)
    total = jnp.zeros((rows, 1), F32)
    scaled = []
    high = back_ref[:, width:span]
    for s in range(2):
        cols = slice(s * half, (s + 1) * half)
        grad = mm(t(0), back_ref[:, cols]) + mm(t(1 + s), high)
        router_cols = router_ref[:, cols]
        grad = grad + mm(p0, router_cols) + mm(p1, router_cols) + mm(p2, router_cols)
        grad = grad * gain_ref[:, cols].astype(F32)
        total += jnp.sum(grad * stored_ref[:, cols].astype(F32), axis=1, keepdims=True)
        scaled.append(grad)
    pull = inverse * inverse * inverse * (total / width)
    for s in range(2):
        cols = slice(s * half, (s + 1) * half)
        value = cotangent_ref[:, cols].astype(F32) + inverse * scaled[s]
        grad_ref[:, cols] = (value - stored_ref[:, cols].astype(F32) * pull).astype(BF16)


def call(kernel, ins, outs, out_specs, scratch=(), sems=0, flops=0, moved=0, limit=60):
    return pl.pallas_call(
        kernel,
        in_specs=ins,
        out_specs=out_specs,
        out_shape=outs,
        scratch_shapes=list(scratch) + ([pltpu.SemaphoreType.DMA((sems,))] if sems else []),
        compiler_params=pltpu.CompilerParams(vmem_limit_bytes=limit * 2**20),
        cost_estimate=pl.CostEstimate(flops=flops, bytes_accessed=moved, transcendentals=0),
    )


def body(
    activations, gradients, stashed, norm_gain, router, gate_weight, up_weight, down_weight, routes_forward, routes_backward
):
    shape = jax.ShapeDtypeStruct
    experts = lax.axis_size("expert")
    rows, width = stashed.shape[1:]
    span = width + width // 2
    inner = gate_weight.shape[3]
    low, slots = experts * LOW, experts * (LOW + HIGH)
    gate_mat, up_mat, down_mat = gate_weight[0, 0], up_weight[0, 0], down_weight[0, 0]
    router_rows, stored = router[0].T, stashed[0]
    routes_f, routes_b = routes_forward[0].T, routes_backward[0].T

    def exchange(block):
        blocks = block.reshape(experts, LOW, block.shape[1])
        return lax.all_to_all(blocks, "expert", split_axis=0, concat_axis=0, tiled=True).reshape(block.shape)

    arrived = passed_along(activations, "section", 1)[0]
    cotangent = passed_along(gradients, "section", -1)[0]

    sent_b = call(
        functools.partial(pack_stored, experts=experts),
        [VMEM] * 3,
        shape((low, span), BF16),
        HBM,
        scratch=[pltpu.VMEM((low, span), BF16)],
        sems=3,
        flops=4 * low * rows * width,
        moved=2**22,
    )(stored, norm_gain, routes_b)
    got_b = exchange(sent_b)
    sent, tables, scalars = call(
        functools.partial(pack_both, experts=experts),
        [VMEM] * 7,
        (shape((low, 2 * span), BF16), shape((rows, 13 * low), BF16), shape((rows, rows), F32)),
        (HBM, VMEM, VMEM),
        scratch=[pltpu.VMEM((low, 2 * span), BF16)],
        sems=6,
        flops=10 * low * rows * width,
        moved=2**23,
    )(stored, cotangent, arrived, norm_gain, router_rows, routes_b, routes_f)
    got = exchange(sent)
    silu, slope, hidden = call(
        functools.partial(expert_stored, sources=experts),
        [VMEM] * 3,
        (shape((slots, inner), F32), shape((slots, inner), F32), shape((slots, inner), BF16)),
        (VMEM,) * 3,
        scratch=[pltpu.VMEM((slots, width), BF16)],
        limit=40,
        flops=4 * slots * width * inner,
        moved=2**24,
    )(got_b, gate_mat, up_mat)
    made = call(
        functools.partial(expert_both, sources=experts),
        [HBM] + [VMEM] * 3 + [HBM] * 3,
        shape((low, 2 * span + 128), BF16),
        HBM,
        scratch=[
            pltpu.VMEM((slots, width), BF16),
            pltpu.VMEM((low, width // 2), BF16),
            pltpu.VMEM((slots, width), BF16),
            pltpu.VMEM((low, width // 2), BF16),
            pltpu.VMEM((width, inner), BF16),
            pltpu.VMEM((width, inner), BF16),
            pltpu.VMEM((inner, width), BF16),
            pltpu.VMEM((slots, inner), BF16),
            pltpu.VMEM((slots, inner), BF16),
            pltpu.VMEM((slots - low, width), BF16),
            pltpu.VMEM((low, 2 * span + 128), BF16),
        ],
        sems=40,
        limit=50,
        flops=12 * slots * width * inner,
        moved=2**24,
    )(got, silu, slope, hidden, gate_mat, up_mat, down_mat)
    back = exchange(made)
    layer_out, input_grad = call(
        functools.partial(combine, experts=experts),
        [VMEM] * 8,
        (shape((rows, width), BF16), shape((rows, width), BF16)),
        (VMEM, VMEM),
        limit=48,
        flops=20 * low * rows * width,
        moved=2**23,
    )(back, tables, scalars, arrived, stored, cotangent, norm_gain, router_rows)
    return layer_out[None], input_grad[None]


def solution(mesh):
    spread_rows = P("section", "expert", None)
    weights = P("section", "expert", None, None)
    placed = (
        spread_rows,
        spread_rows,
        spread_rows,
        P("section", None),
        P("section", None, None),
        weights,
        weights,
        weights,
        spread_rows,
        spread_rows,
    )
    return jax.shard_map(body, mesh=mesh, in_specs=placed, out_specs=(spread_rows, spread_rows), check_vma=False)
```

```python
import functools

import jax
import jax.numpy as jnp
from jax import lax
from jax.experimental import pallas as pl
from jax.experimental.pallas import tpu as pltpu
from jax.sharding import PartitionSpec as P


NORM_EPS = 1e-06
LOW = 8
HIGH = 4
F32 = jnp.float32
BF16 = jnp.bfloat16
NT = (((1,), (1,)), ((), ()))
ANY = pl.BlockSpec(memory_space=pl.ANY)
HBM = pl.BlockSpec(memory_space=pltpu.HBM)
VMEM = pl.BlockSpec(memory_space=pltpu.VMEM)


def passed_along(value, axis, steps):
    count = lax.axis_size(axis)
    pairs = [(source, (source + steps) % count) for source in range(count)]
    return lax.ppermute(value, axis, pairs)


def mm(a, b):
    return jnp.dot(a, b, preferred_element_type=F32)


def mm_nt(a, b):
    return lax.dot_general(a, b, NT, preferred_element_type=F32)


def iota(shape, dim):
    return lax.broadcasted_iota(jnp.int32, shape, dim)


def mask(condition):
    return condition.astype(F32).astype(BF16)


class Copies:
    def __init__(self, sems):
        self.sems = sems
        self.used = 0

    def start(self, source, target):
        copy = pltpu.make_async_copy(source, target, self.sems.at[self.used])
        self.used += 1
        copy.start()
        return copy


def normalized(tokens, gain_row):
    values = tokens.astype(F32)
    inverse = lax.rsqrt(jnp.mean(values * values, axis=-1, keepdims=True) + NORM_EPS)
    return (values * inverse * gain_row.astype(F32)).astype(BF16), inverse


def places(routes, experts):
    count = routes.shape[1]
    experts_at = iota((experts, count), 0)
    matches = [routes[k : k + 1, :] == experts_at for k in range(2)]
    named = mask(matches[0] | matches[1])
    earlier = mm(named, mask(iota((count, count), 0) < iota((count, count), 1)))
    found = []
    for k in range(2):
        slot = jnp.sum(jnp.where(matches[k], earlier, 0.0), axis=0, keepdims=True).astype(jnp.int32)
        base = routes[k : k + 1, :] * LOW
        whole = jnp.where(slot < LOW, base + slot, -LOW)
        half = jnp.where(slot < LOW, -LOW, base + slot - LOW)
        found.append((whole, half, matches[k]))
    return found


def spots_of(found):
    (w0, h0, _), (w1, h1, _) = found
    return (w0, w1), (h0, h1), (h0 + HIGH, h1 + HIGH)


def table(at, spots, scales=(1.0, 1.0)):
    total = jnp.where(at == spots[0], scales[0], 0.0)
    return total + jnp.where(at == spots[1], scales[1], 0.0)


def pack(tokens, tables, made_ref, out_ref, at, copies):
    whole, left, right = (t.astype(BF16) for t in tables)
    half = tokens.shape[1] // 2
    running = []

    def give(value, column):
        cols = slice(at + column, at + column + half)
        made_ref[:, cols] = value.astype(BF16)
        running.append(copies.start(made_ref.at[:, cols], out_ref.at[:, cols]))

    give(mm(whole, tokens[:, :half]), 0)
    give(mm(whole, tokens[:, half:]), half)
    give(mm(left, tokens[:, :half]) + mm(right, tokens[:, half:]), 2 * half)
    return running


def pack_stored(stored_ref, gain_ref, routes_ref, out_ref, made_ref, sems, *, experts):
    found = places(routes_ref[...], experts)
    at = iota((experts * LOW, routes_ref.shape[1]), 0)
    normed, _ = normalized(stored_ref[...], gain_ref[...])
    for copy in pack(normed, [table(at, s) for s in spots_of(found)], made_ref, out_ref, 0, Copies(sems)):
        copy.wait()


def weights_of(normed, router_rows, found):
    logits = mm_nt(router_rows, normed)
    sig = [
        jax.nn.sigmoid(jnp.sum(jnp.where(match, logits, 0.0), axis=0, keepdims=True))
        for _, _, match in found
    ]
    total = sig[0] + sig[1]
    return [s / total for s in sig], sig


def split(value):
    high = value.astype(BF16)
    return high, (value - high.astype(F32)).astype(BF16)


def pack_both(
    stored_ref, cotangent_ref, arrived_ref, gain_ref, router_ref, routes_b_ref, routes_f_ref,
    out_ref, tables_ref, scalars_ref, made_ref, sems, *, experts,
):
    gain_row = gain_ref[...]
    router_rows = router_ref[...]
    rows, width = stored_ref.shape
    span = experts * LOW
    at = iota((span, rows), 0)
    copies = Copies(sems)

    normed_b, inverse_b = normalized(stored_ref[...], gain_row)
    found_b = places(routes_b_ref[...], experts)
    weights_b, sig_b = weights_of(normed_b, router_rows, found_b)
    scales = [w.astype(BF16).astype(F32) for w in weights_b]
    spots_b = spots_of(found_b)
    running = pack(cotangent_ref[...], [table(at, s, scales) for s in spots_b], made_ref, out_ref, 0, copies)
    normed_f, _ = normalized(arrived_ref[...], gain_row)
    found_f = places(routes_f_ref[...], experts)
    spots_f = spots_of(found_f)
    running += pack(normed_f, [table(at, s) for s in spots_f], made_ref, out_ref, width + width // 2, copies)
    weights_f, _ = weights_of(normed_f, router_rows, found_f)

    kept = [table(at, s) for s in spots_b]
    kept += [jnp.where(at == s, 1.0, 0.0) for s in (*spots_b[0], *spots_b[1])]
    for s in spots_f:
        kept += [part.astype(F32) for part in split(table(at, s, weights_f))]
    for i, value in enumerate(kept):
        tables_ref[:, i * span : (i + 1) * span] = value.T.astype(BF16)

    ratio = [jnp.where(s > 0.0, w / s, 1.0) for w, s in zip(weights_b, scales)]
    routes_b = routes_b_ref[...].astype(F32)
    lines = [*weights_b, *sig_b, *ratio, routes_b[0:1], routes_b[1:2]]
    line_at = iota((rows, rows), 0)
    scalars = jnp.zeros((rows, rows), F32)
    for i, value in enumerate(lines):
        scalars = jnp.where(line_at == i, value, scalars)
    scalars_ref[...] = jnp.where(iota((rows, rows), 1) == len(lines), inverse_b, scalars.T)
    for copy in running:
        copy.wait()


def half_places(count):
    i = iota((count * HIGH, count * LOW), 0)
    j = iota((count * HIGH, count * LOW), 1)
    left = 2 * i - (i & (HIGH - 1))
    return mask(j == left), mask(j == left + HIGH)


def half_homes(count):
    i = iota((count * LOW, count * HIGH), 1)
    j = iota((count * LOW, count * HIGH), 0)
    left = 2 * i - (i & (HIGH - 1))
    return mask(j == left), mask(j == left + HIGH)


def join_halves(rows_ref, part, sources):
    low = sources * LOW
    half = rows_ref.shape[1] // 2
    take_left, take_right = half_places(sources)
    rows_ref[low:, :half] = mm(take_left, part).astype(BF16)
    rows_ref[low:, half:] = mm(take_right, part).astype(BF16)


def expert_stored(block_ref, gate_ref, up_ref, gated_ref, upper_ref, rows_ref, *, sources):
    low = sources * LOW
    width = rows_ref.shape[1]
    rows_ref[:low, :] = block_ref[:, :width]
    join_halves(rows_ref, block_ref[:, width:], sources)
    rows = rows_ref[...]
    for f in range(0, gate_ref.shape[1], 256):
        gated_ref[:, f : f + 256] = mm(rows, gate_ref[:, f : f + 256])
        upper_ref[:, f : f + 256] = mm(rows, up_ref[:, f : f + 256])


def expert_both(
    block_any, gated_any, upper_any, gate_any, up_any, down_any, out_any,
    gated_ref, upper_ref, rows_b, half_b, rows_f, half_f, gate_ref, up_ref, down_ref, grad_gate_ref, grad_up_ref, made_ref, out_ref, sems,
    *, sources,
):
    low = sources * LOW
    width = rows_b.shape[1]
    half = width // 2
    span = width + half
    inner = gate_ref.shape[1]
    step = 256
    wide = 512
    copies = Copies(sems)

    def started(source, target, step):
        count = target.shape[0]
        return [copies.start(source.at[i : i + step, :], target.at[i : i + step, :]) for i in range(0, count, step)]

    def taken(running):
        for copy in running:
            copy.wait()

    first = [
        copies.start(block_any.at[:, width:span], half_b),
        copies.start(block_any.at[:, :width], rows_b.at[:low, :]),
        *started(down_any, down_ref, inner // 2),
    ]
    held = [copies.start(gated_any, gated_ref), copies.start(upper_any, upper_ref)]
    taken(first[:2])
    second = started(gate_any, gate_ref, width // 2)
    join_halves(rows_b, half_b[...], sources)
    taken(first[2:])
    second += started(up_any, up_ref, width // 2)
    scores = jnp.zeros((rows_b.shape[0], 1), F32)
    for f in range(0, inner, step):
        cols = slice(f, f + step)
        grad_hidden = mm_nt(rows_b[...], down_ref[cols, :])
        if f == 0:
            taken(held)
        gated = gated_ref[:, cols]
        upper = upper_ref[:, cols]
        sig = jax.nn.sigmoid(gated)
        silu = gated * sig
        hidden = (silu * upper).astype(BF16).astype(F32)
        scores += jnp.sum(grad_hidden * hidden, axis=1, keepdims=True)
        grad_up_ref[:, cols] = (grad_hidden * silu).astype(BF16)
        slope = upper * sig * (1.0 + gated * (1.0 - sig))
        grad_gate_ref[:, cols] = (grad_hidden * slope).astype(BF16)

    put_left, _ = half_homes(sources)
    at = iota((low, 128), 1)
    high, rest = split(scores)
    tail = jnp.where(at == 0, high[:low].astype(F32), jnp.where(at == 1, rest[:low].astype(F32), 0.0))
    at = iota((low // 2, 128), 1)
    more = jnp.where(at == 2, high[low:].astype(F32), jnp.where(at == 3, rest[low:].astype(F32), 0.0))
    out_ref[:, 2 * span :] = (tail + mm(put_left, more.astype(BF16))).astype(BF16)
    given = [copies.start(out_ref.at[:, 2 * span :], out_any.at[:, 2 * span :])]

    def give(columns):
        given.append(copies.start(out_ref.at[:, columns], out_any.at[:, columns]))

    def give_halves(base):
        put_left, put_right = half_homes(sources)
        both = mm(put_left, made_ref[:, :half]) + mm(put_right, made_ref[:, half:])
        out_ref[:, base + width : base + span] = both.astype(BF16)
        give(slice(base + width, base + span))

    taken(second)
    third = [
        copies.start(block_any.at[:, span + width :], half_f),
        copies.start(block_any.at[:, span : span + width], rows_f.at[:low, :]),
    ]
    for n in range(0, width, wide):
        cols = slice(n, n + wide)
        made = (mm_nt(grad_gate_ref[...], gate_ref[cols, :]) + mm_nt(grad_up_ref[...], up_ref[cols, :])).astype(BF16)
        out_ref[:, cols] = made[:low]
        made_ref[:, cols] = made[low:]
        give(cols)
    give_halves(0)

    taken(third)
    join_halves(rows_f, half_f[...], sources)
    for f in range(0, inner, step):
        gate = mm(rows_f[...], gate_ref[:, f : f + step])
        up = mm(rows_f[...], up_ref[:, f : f + step])
        grad_up_ref[:, f : f + step] = (gate * jax.nn.sigmoid(gate) * up).astype(BF16)
    for n in range(0, width, wide):
        made = mm(grad_up_ref[...], down_ref[:, n : n + wide]).astype(BF16)
        cols = slice(span + n, span + n + wide)
        out_ref[:, cols] = made[:low]
        made_ref[:, n : n + wide] = made[low:]
        give(cols)
    give_halves(span)
    for copy in given:
        copy.wait()


def combine(
    back_ref, tables_ref, scalars_ref, arrived_ref, stored_ref, cotangent_ref, gain_ref, router_ref, layer_ref, grad_ref,
    *, experts,
):
    rows, width = arrived_ref.shape
    half = width // 2
    span = width + half
    slots = experts * LOW

    def t(i):
        return tables_ref[:, i * slots : (i + 1) * slots]

    high = back_ref[:, span + width : 2 * span]
    for s, side in ((0, 9), (1, 11)):
        cols = slice(s * half, (s + 1) * half)
        low = back_ref[:, span + s * half : span + (s + 1) * half]
        mixed = mm(t(7), low) + mm(t(8), low) + mm(t(side), high) + mm(t(side + 1), high)
        layer_ref[:, cols] = (arrived_ref[:, cols].astype(F32) + mixed).astype(BF16)

    w0, w1, s0, s1, r0, r1, e0, e1, inverse = (scalars_ref[:, i : i + 1] for i in range(9))
    extra = back_ref[:, 2 * span : 2 * span + 128]
    u = []
    for k, ratio in ((0, r0), (1, r1)):
        got = mm(t(3 + k), extra)
        more = mm(t(5 + k), extra)
        u.append((got[:, 0:1] + got[:, 1:2] + more[:, 2:3] + more[:, 3:4]) * ratio)
    cross = u[0] * w1 - w0 * u[1]
    expert_at = iota((rows, experts), 1).astype(F32)
    picks = jnp.where(e0 == expert_at, cross * (1.0 - s0), 0.0)
    picks = picks - jnp.where(e1 == expert_at, cross * (1.0 - s1), 0.0)
    p0, p1 = split(picks)
    p2 = (picks - p0.astype(F32) - p1.astype(F32)).astype(BF16)
    total = jnp.zeros((rows, 1), F32)
    scaled = []
    high = back_ref[:, width:span]
    for s in range(2):
        cols = slice(s * half, (s + 1) * half)
        grad = mm(t(0), back_ref[:, cols]) + mm(t(1 + s), high)
        router_cols = router_ref[:, cols]
        grad = grad + mm(p0, router_cols) + mm(p1, router_cols) + mm(p2, router_cols)
        grad = grad * gain_ref[:, cols].astype(F32)
        total += jnp.sum(grad * stored_ref[:, cols].astype(F32), axis=1, keepdims=True)
        scaled.append(grad)
    pull = inverse * inverse * inverse * (total / width)
    for s in range(2):
        cols = slice(s * half, (s + 1) * half)
        value = cotangent_ref[:, cols].astype(F32) + inverse * scaled[s]
        grad_ref[:, cols] = (value - stored_ref[:, cols].astype(F32) * pull).astype(BF16)


def call(kernel, ins, outs, out_specs, scratch=(), sems=0, flops=0, moved=0, limit=60):
    return pl.pallas_call(
        kernel,
        in_specs=ins,
        out_specs=out_specs,
        out_shape=outs,
        scratch_shapes=list(scratch) + ([pltpu.SemaphoreType.DMA((sems,))] if sems else []),
        compiler_params=pltpu.CompilerParams(vmem_limit_bytes=limit * 2**20),
        cost_estimate=pl.CostEstimate(flops=flops, bytes_accessed=moved, transcendentals=0),
    )


def body(
    activations, gradients, stashed, norm_gain, router, gate_weight, up_weight, down_weight, routes_forward, routes_backward
):
    shape = jax.ShapeDtypeStruct
    experts = lax.axis_size("expert")
    rows, width = stashed.shape[1:]
    span = width + width // 2
    inner = gate_weight.shape[3]
    low, slots = experts * LOW, experts * (LOW + HIGH)
    gate_mat, up_mat, down_mat = gate_weight[0, 0], up_weight[0, 0], down_weight[0, 0]
    router_rows, stored = router[0].T, stashed[0]
    routes_f, routes_b = routes_forward[0].T, routes_backward[0].T

    def exchange(block):
        blocks = block.reshape(experts, LOW, block.shape[1])
        return lax.all_to_all(blocks, "expert", split_axis=0, concat_axis=0, tiled=True).reshape(block.shape)

    arrived = passed_along(activations, "section", 1)[0]
    cotangent = passed_along(gradients, "section", -1)[0]

    sent_b = call(
        functools.partial(pack_stored, experts=experts),
        [VMEM] * 3,
        shape((low, span), BF16),
        HBM,
        scratch=[pltpu.VMEM((low, span), BF16)],
        sems=3,
        flops=4 * low * rows * width,
        moved=2**22,
    )(stored, norm_gain, routes_b)
    got_b = exchange(sent_b)
    sent, tables, scalars = call(
        functools.partial(pack_both, experts=experts),
        [VMEM] * 7,
        (shape((low, 2 * span), BF16), shape((rows, 13 * low), BF16), shape((rows, rows), F32)),
        (HBM, VMEM, VMEM),
        scratch=[pltpu.VMEM((low, 2 * span), BF16)],
        sems=6,
        flops=10 * low * rows * width,
        moved=2**23,
    )(stored, cotangent, arrived, norm_gain, router_rows, routes_b, routes_f)
    got = exchange(sent)
    gated, upper = call(
        functools.partial(expert_stored, sources=experts),
        [VMEM] * 3,
        (shape((slots, inner), F32), shape((slots, inner), F32)),
        (VMEM, VMEM),
        scratch=[pltpu.VMEM((slots, width), BF16)],
        limit=40,
        flops=4 * slots * width * inner,
        moved=2**24,
    )(got_b, gate_mat, up_mat)
    made = call(
        functools.partial(expert_both, sources=experts),
        [HBM] * 6,
        shape((low, 2 * span + 128), BF16),
        HBM,
        scratch=[
            pltpu.VMEM((slots, inner), F32),
            pltpu.VMEM((slots, inner), F32),
            pltpu.VMEM((slots, width), BF16),
            pltpu.VMEM((low, width // 2), BF16),
            pltpu.VMEM((slots, width), BF16),
            pltpu.VMEM((low, width // 2), BF16),
            pltpu.VMEM((width, inner), BF16),
            pltpu.VMEM((width, inner), BF16),
            pltpu.VMEM((inner, width), BF16),
            pltpu.VMEM((slots, inner), BF16),
            pltpu.VMEM((slots, inner), BF16),
            pltpu.VMEM((slots - low, width), BF16),
            pltpu.VMEM((low, 2 * span + 128), BF16),
        ],
        sems=40,
        limit=54,
        flops=12 * slots * width * inner,
        moved=2**24,
    )(got, gated, upper, gate_mat, up_mat, down_mat)
    back = exchange(made)
    layer_out, input_grad = call(
        functools.partial(combine, experts=experts),
        [VMEM] * 8,
        (shape((rows, width), BF16), shape((rows, width), BF16)),
        (VMEM, VMEM),
        limit=48,
        flops=20 * low * rows * width,
        moved=2**23,
    )(back, tables, scalars, arrived, stored, cotangent, norm_gain, router_rows)
    return layer_out[None], input_grad[None]


def solution(mesh):
    spread_rows = P("section", "expert", None)
    weights = P("section", "expert", None, None)
    placed = (
        spread_rows,
        spread_rows,
        spread_rows,
        P("section", None),
        P("section", None, None),
        weights,
        weights,
        weights,
        spread_rows,
        spread_rows,
    )
    return jax.shard_map(body, mesh=mesh, in_specs=placed, out_specs=(spread_rows, spread_rows), check_vma=False)
```

```python
import functools

import jax
import jax.numpy as jnp
from jax import lax
from jax.experimental import pallas as pl
from jax.experimental.pallas import tpu as pltpu
from jax.sharding import PartitionSpec as P


NORM_EPS = 1e-06
LOW = 8
HIGH = 4
F32 = jnp.float32
BF16 = jnp.bfloat16
NT = (((1,), (1,)), ((), ()))
ANY = pl.BlockSpec(memory_space=pl.ANY)
HBM = pl.BlockSpec(memory_space=pltpu.HBM)
VMEM = pl.BlockSpec(memory_space=pltpu.VMEM)


def passed_along(value, axis, steps):
    count = lax.axis_size(axis)
    pairs = [(source, (source + steps) % count) for source in range(count)]
    return lax.ppermute(value, axis, pairs)


def mm(a, b):
    return jnp.dot(a, b, preferred_element_type=F32)


def mm_nt(a, b):
    return lax.dot_general(a, b, NT, preferred_element_type=F32)


def iota(shape, dim):
    return lax.broadcasted_iota(jnp.int32, shape, dim)


def mask(condition):
    return condition.astype(F32).astype(BF16)


class Copies:
    def __init__(self, sems):
        self.sems = sems
        self.used = 0

    def start(self, source, target):
        copy = pltpu.make_async_copy(source, target, self.sems.at[self.used])
        self.used += 1
        copy.start()
        return copy


def normalized(tokens, gain_row):
    values = tokens.astype(F32)
    inverse = lax.rsqrt(jnp.mean(values * values, axis=-1, keepdims=True) + NORM_EPS)
    return (values * inverse * gain_row.astype(F32)).astype(BF16), inverse


def places(routes, experts):
    count = routes.shape[1]
    experts_at = iota((experts, count), 0)
    matches = [routes[k : k + 1, :] == experts_at for k in range(2)]
    named = mask(matches[0] | matches[1])
    earlier = mm(named, mask(iota((count, count), 0) < iota((count, count), 1)))
    found = []
    for k in range(2):
        slot = jnp.sum(jnp.where(matches[k], earlier, 0.0), axis=0, keepdims=True).astype(jnp.int32)
        base = routes[k : k + 1, :] * LOW
        whole = jnp.where(slot < LOW, base + slot, -LOW)
        half = jnp.where(slot < LOW, -LOW, base + slot - LOW)
        found.append((whole, half, matches[k]))
    return found


def spots_of(found):
    (w0, h0, _), (w1, h1, _) = found
    return (w0, w1), (h0, h1), (h0 + HIGH, h1 + HIGH)


def table(at, spots, scales=(1.0, 1.0)):
    total = jnp.where(at == spots[0], scales[0], 0.0)
    return total + jnp.where(at == spots[1], scales[1], 0.0)


def pack(tokens, tables, made_ref, out_ref, at, copies):
    whole, left, right = (t.astype(BF16) for t in tables)
    half = tokens.shape[1] // 2
    running = []

    def give(value, column):
        cols = slice(at + column, at + column + half)
        made_ref[:, cols] = value.astype(BF16)
        running.append(copies.start(made_ref.at[:, cols], out_ref.at[:, cols]))

    give(mm(whole, tokens[:, :half]), 0)
    give(mm(whole, tokens[:, half:]), half)
    give(mm(left, tokens[:, :half]) + mm(right, tokens[:, half:]), 2 * half)
    return running


def pack_stored(stored_ref, gain_ref, routes_ref, out_ref, made_ref, sems, *, experts):
    found = places(routes_ref[...], experts)
    at = iota((experts * LOW, routes_ref.shape[1]), 0)
    normed, _ = normalized(stored_ref[...], gain_ref[...])
    for copy in pack(normed, [table(at, s) for s in spots_of(found)], made_ref, out_ref, 0, Copies(sems)):
        copy.wait()


def weights_of(normed, router_rows, found):
    logits = mm_nt(router_rows, normed)
    sig = [
        jax.nn.sigmoid(jnp.sum(jnp.where(match, logits, 0.0), axis=0, keepdims=True))
        for _, _, match in found
    ]
    total = sig[0] + sig[1]
    return [s / total for s in sig], sig


def split(value):
    high = value.astype(BF16)
    return high, (value - high.astype(F32)).astype(BF16)


def save(kept, tables_ref, span):
    for i, value in enumerate(kept):
        tables_ref[:, i * span : (i + 1) * span] = value.T.astype(BF16)


def prepare_stored(
    stored_ref, gain_ref, router_ref, routes_ref, scaled_ref, tables_ref, scalars_ref, *, experts,
):
    rows = stored_ref.shape[0]
    span = experts * LOW
    at = iota((span, rows), 0)
    normed, inverse = normalized(stored_ref[...], gain_ref[...])
    found = places(routes_ref[...], experts)
    weights, sig = weights_of(normed, router_ref[...], found)
    scales = [w.astype(BF16).astype(F32) for w in weights]
    spots = spots_of(found)
    for i, s in enumerate(spots):
        scaled_ref[:, i * rows : (i + 1) * rows] = table(at, s, scales).astype(BF16)
    kept = [table(at, s) for s in spots]
    kept += [jnp.where(at == s, 1.0, 0.0) for s in (*spots[0], *spots[1])]
    save(kept, tables_ref, span)
    ratio = [jnp.where(s > 0.0, w / s, 1.0) for w, s in zip(weights, scales)]
    routes = routes_ref[...].astype(F32)
    lines = [*weights, *sig, *ratio, routes[0:1], routes[1:2]]
    line_at = iota((rows, rows), 0)
    scalars = jnp.zeros((rows, rows), F32)
    for i, value in enumerate(lines):
        scalars = jnp.where(line_at == i, value, scalars)
    scalars_ref[...] = jnp.where(iota((rows, rows), 1) == len(lines), inverse, scalars.T)


def prepare_front(arrived_ref, gain_ref, router_ref, routes_ref, tables_ref, *, experts):
    rows = arrived_ref.shape[0]
    span = experts * LOW
    at = iota((span, rows), 0)
    normed, _ = normalized(arrived_ref[...], gain_ref[...])
    found = places(routes_ref[...], experts)
    weights, _ = weights_of(normed, router_ref[...], found)
    kept = []
    for s in spots_of(found):
        kept += [part.astype(F32) for part in split(table(at, s, weights))]
    save(kept, tables_ref, span)


def pack_both(
    cotangent_ref, arrived_ref, gain_ref, routes_ref, scaled_ref, out_ref, made_ref, sems, *, experts,
):
    rows, width = arrived_ref.shape
    at = iota((experts * LOW, rows), 0)
    copies = Copies(sems)
    scaled = [scaled_ref[:, i * rows : (i + 1) * rows] for i in range(3)]
    running = pack(cotangent_ref[...], scaled, made_ref, out_ref, 0, copies)
    normed, _ = normalized(arrived_ref[...], gain_ref[...])
    tables = [table(at, s) for s in spots_of(places(routes_ref[...], experts))]
    running += pack(normed, tables, made_ref, out_ref, width + width // 2, copies)
    for copy in running:
        copy.wait()


def half_places(count):
    i = iota((count * HIGH, count * LOW), 0)
    j = iota((count * HIGH, count * LOW), 1)
    left = 2 * i - (i & (HIGH - 1))
    return mask(j == left), mask(j == left + HIGH)


def half_homes(count):
    i = iota((count * LOW, count * HIGH), 1)
    j = iota((count * LOW, count * HIGH), 0)
    left = 2 * i - (i & (HIGH - 1))
    return mask(j == left), mask(j == left + HIGH)


def join_halves(rows_ref, part, sources):
    low = sources * LOW
    half = rows_ref.shape[1] // 2
    take_left, take_right = half_places(sources)
    rows_ref[low:, :half] = mm(take_left, part).astype(BF16)
    rows_ref[low:, half:] = mm(take_right, part).astype(BF16)


def expert_stored(block_ref, gate_ref, up_ref, gated_ref, upper_ref, rows_ref, *, sources):
    low = sources * LOW
    width = rows_ref.shape[1]
    rows_ref[:low, :] = block_ref[:, :width]
    join_halves(rows_ref, block_ref[:, width:], sources)
    rows = rows_ref[...]
    for f in range(0, gate_ref.shape[1], 256):
        gated_ref[:, f : f + 256] = mm(rows, gate_ref[:, f : f + 256])
        upper_ref[:, f : f + 256] = mm(rows, up_ref[:, f : f + 256])


def expert_both(
    block_any, gated_any, upper_any, gate_any, up_any, down_any, out_any,
    gated_ref, upper_ref, rows_b, half_b, rows_f, half_f, gate_ref, up_ref, down_ref, grad_gate_ref, grad_up_ref, made_ref, out_ref, sems,
    *, sources,
):
    low = sources * LOW
    width = rows_b.shape[1]
    half = width // 2
    span = width + half
    inner = gate_ref.shape[1]
    step = 256
    wide = 512
    copies = Copies(sems)

    def started(source, target, step):
        count = target.shape[0]
        return [copies.start(source.at[i : i + step, :], target.at[i : i + step, :]) for i in range(0, count, step)]

    def taken(running):
        for copy in running:
            copy.wait()

    first = [
        copies.start(block_any.at[:, width:span], half_b),
        copies.start(block_any.at[:, :width], rows_b.at[:low, :]),
        *started(down_any, down_ref, inner // 2),
    ]
    held = [copies.start(gated_any, gated_ref), copies.start(upper_any, upper_ref)]
    taken(first[:2])
    second = started(gate_any, gate_ref, width // 2)
    join_halves(rows_b, half_b[...], sources)
    taken(first[2:])
    second += started(up_any, up_ref, width // 2)
    scores = jnp.zeros((rows_b.shape[0], 1), F32)
    for f in range(0, inner, step):
        cols = slice(f, f + step)
        grad_hidden = mm_nt(rows_b[...], down_ref[cols, :])
        if f == 0:
            taken(held)
        gated = gated_ref[:, cols]
        upper = upper_ref[:, cols]
        sig = jax.nn.sigmoid(gated)
        silu = gated * sig
        hidden = (silu * upper).astype(BF16).astype(F32)
        scores += jnp.sum(grad_hidden * hidden, axis=1, keepdims=True)
        grad_up_ref[:, cols] = (grad_hidden * silu).astype(BF16)
        slope = upper * sig * (1.0 + gated * (1.0 - sig))
        grad_gate_ref[:, cols] = (grad_hidden * slope).astype(BF16)

    put_left, _ = half_homes(sources)
    at = iota((low, 128), 1)
    high, rest = split(scores)
    tail = jnp.where(at == 0, high[:low].astype(F32), jnp.where(at == 1, rest[:low].astype(F32), 0.0))
    at = iota((low // 2, 128), 1)
    more = jnp.where(at == 2, high[low:].astype(F32), jnp.where(at == 3, rest[low:].astype(F32), 0.0))
    out_ref[:, 2 * span :] = (tail + mm(put_left, more.astype(BF16))).astype(BF16)
    given = [copies.start(out_ref.at[:, 2 * span :], out_any.at[:, 2 * span :])]

    def give(columns):
        given.append(copies.start(out_ref.at[:, columns], out_any.at[:, columns]))

    def give_halves(base):
        put_left, put_right = half_homes(sources)
        both = mm(put_left, made_ref[:, :half]) + mm(put_right, made_ref[:, half:])
        out_ref[:, base + width : base + span] = both.astype(BF16)
        give(slice(base + width, base + span))

    taken(second)
    third = [
        copies.start(block_any.at[:, span + width :], half_f),
        copies.start(block_any.at[:, span : span + width], rows_f.at[:low, :]),
    ]
    for n in range(0, width, wide):
        cols = slice(n, n + wide)
        made = (mm_nt(grad_gate_ref[...], gate_ref[cols, :]) + mm_nt(grad_up_ref[...], up_ref[cols, :])).astype(BF16)
        out_ref[:, cols] = made[:low]
        made_ref[:, cols] = made[low:]
        give(cols)
    give_halves(0)

    taken(third)
    join_halves(rows_f, half_f[...], sources)
    for f in range(0, inner, step):
        gate = mm(rows_f[...], gate_ref[:, f : f + step])
        up = mm(rows_f[...], up_ref[:, f : f + step])
        grad_up_ref[:, f : f + step] = (gate * jax.nn.sigmoid(gate) * up).astype(BF16)
    for n in range(0, width, wide):
        made = mm(grad_up_ref[...], down_ref[:, n : n + wide]).astype(BF16)
        cols = slice(span + n, span + n + wide)
        out_ref[:, cols] = made[:low]
        made_ref[:, n : n + wide] = made[low:]
        give(cols)
    give_halves(span)
    for copy in given:
        copy.wait()


def combine(
    back_ref, front_ref, tables_ref, scalars_ref, arrived_ref, stored_ref, cotangent_ref, gain_ref, router_ref,
    layer_ref, grad_ref,
    *, experts,
):
    rows, width = arrived_ref.shape
    half = width // 2
    span = width + half
    slots = experts * LOW

    def t(i):
        return tables_ref[:, i * slots : (i + 1) * slots]

    def w(i):
        return front_ref[:, i * slots : (i + 1) * slots]

    high = back_ref[:, span + width : 2 * span]
    for s, side in ((0, 2), (1, 4)):
        cols = slice(s * half, (s + 1) * half)
        low = back_ref[:, span + s * half : span + (s + 1) * half]
        mixed = mm(w(0), low) + mm(w(1), low) + mm(w(side), high) + mm(w(side + 1), high)
        layer_ref[:, cols] = (arrived_ref[:, cols].astype(F32) + mixed).astype(BF16)

    w0, w1, s0, s1, r0, r1, e0, e1, inverse = (scalars_ref[:, i : i + 1] for i in range(9))
    extra = back_ref[:, 2 * span : 2 * span + 128]
    u = []
    for k, ratio in ((0, r0), (1, r1)):
        got = mm(t(3 + k), extra)
        more = mm(t(5 + k), extra)
        u.append((got[:, 0:1] + got[:, 1:2] + more[:, 2:3] + more[:, 3:4]) * ratio)
    cross = u[0] * w1 - w0 * u[1]
    expert_at = iota((rows, experts), 1).astype(F32)
    picks = jnp.where(e0 == expert_at, cross * (1.0 - s0), 0.0)
    picks = picks - jnp.where(e1 == expert_at, cross * (1.0 - s1), 0.0)
    p0, p1 = split(picks)
    p2 = (picks - p0.astype(F32) - p1.astype(F32)).astype(BF16)
    total = jnp.zeros((rows, 1), F32)
    scaled = []
    high = back_ref[:, width:span]
    for s in range(2):
        cols = slice(s * half, (s + 1) * half)
        grad = mm(t(0), back_ref[:, cols]) + mm(t(1 + s), high)
        router_cols = router_ref[:, cols]
        grad = grad + mm(p0, router_cols) + mm(p1, router_cols) + mm(p2, router_cols)
        grad = grad * gain_ref[:, cols].astype(F32)
        total += jnp.sum(grad * stored_ref[:, cols].astype(F32), axis=1, keepdims=True)
        scaled.append(grad)
    pull = inverse * inverse * inverse * (total / width)
    for s in range(2):
        cols = slice(s * half, (s + 1) * half)
        value = cotangent_ref[:, cols].astype(F32) + inverse * scaled[s]
        grad_ref[:, cols] = (value - stored_ref[:, cols].astype(F32) * pull).astype(BF16)


def call(kernel, ins, outs, out_specs, scratch=(), sems=0, flops=0, moved=0, limit=60):
    return pl.pallas_call(
        kernel,
        in_specs=ins,
        out_specs=out_specs,
        out_shape=outs,
        scratch_shapes=list(scratch) + ([pltpu.SemaphoreType.DMA((sems,))] if sems else []),
        compiler_params=pltpu.CompilerParams(vmem_limit_bytes=limit * 2**20),
        cost_estimate=pl.CostEstimate(flops=flops, bytes_accessed=moved, transcendentals=0),
    )


def body(
    activations, gradients, stashed, norm_gain, router, gate_weight, up_weight, down_weight, routes_forward, routes_backward
):
    shape = jax.ShapeDtypeStruct
    experts = lax.axis_size("expert")
    rows, width = stashed.shape[1:]
    span = width + width // 2
    inner = gate_weight.shape[3]
    low, slots = experts * LOW, experts * (LOW + HIGH)
    gate_mat, up_mat, down_mat = gate_weight[0, 0], up_weight[0, 0], down_weight[0, 0]
    router_rows, stored = router[0].T, stashed[0]
    routes_f, routes_b = routes_forward[0].T, routes_backward[0].T

    def exchange(block):
        blocks = block.reshape(experts, LOW, block.shape[1])
        return lax.all_to_all(blocks, "expert", split_axis=0, concat_axis=0, tiled=True).reshape(block.shape)

    arrived = passed_along(activations, "section", 1)[0]
    cotangent = passed_along(gradients, "section", -1)[0]

    sent_b = call(
        functools.partial(pack_stored, experts=experts),
        [VMEM] * 3,
        shape((low, span), BF16),
        HBM,
        scratch=[pltpu.VMEM((low, span), BF16)],
        sems=3,
        flops=4 * low * rows * width,
        moved=2**22,
    )(stored, norm_gain, routes_b)
    got_b = exchange(sent_b)
    scaled, tables, scalars = call(
        functools.partial(prepare_stored, experts=experts),
        [VMEM] * 4,
        (shape((low, 3 * rows), BF16), shape((rows, 7 * low), BF16), shape((rows, rows), F32)),
        (VMEM,) * 3,
        flops=4 * low * rows * width,
        moved=2**21,
    )(stored, norm_gain, router_rows, routes_b)
    sent = call(
        functools.partial(pack_both, experts=experts),
        [VMEM] * 5,
        shape((low, 2 * span), BF16),
        HBM,
        scratch=[pltpu.VMEM((low, 2 * span), BF16)],
        sems=6,
        flops=10 * low * rows * width,
        moved=2**23,
    )(cotangent, arrived, norm_gain, routes_f, scaled)
    front = call(
        functools.partial(prepare_front, experts=experts),
        [VMEM] * 4,
        shape((rows, 6 * low), BF16),
        VMEM,
        flops=4 * low * rows * width,
        moved=2**21,
    )(arrived, norm_gain, router_rows, routes_f)
    got = exchange(sent)
    gated, upper = call(
        functools.partial(expert_stored, sources=experts),
        [VMEM] * 3,
        (shape((slots, inner), F32), shape((slots, inner), F32)),
        (VMEM, VMEM),
        scratch=[pltpu.VMEM((slots, width), BF16)],
        limit=40,
        flops=4 * slots * width * inner,
        moved=2**24,
    )(got_b, gate_mat, up_mat)
    made = call(
        functools.partial(expert_both, sources=experts),
        [HBM] * 6,
        shape((low, 2 * span + 128), BF16),
        HBM,
        scratch=[
            pltpu.VMEM((slots, inner), F32),
            pltpu.VMEM((slots, inner), F32),
            pltpu.VMEM((slots, width), BF16),
            pltpu.VMEM((low, width // 2), BF16),
            pltpu.VMEM((slots, width), BF16),
            pltpu.VMEM((low, width // 2), BF16),
            pltpu.VMEM((width, inner), BF16),
            pltpu.VMEM((width, inner), BF16),
            pltpu.VMEM((inner, width), BF16),
            pltpu.VMEM((slots, inner), BF16),
            pltpu.VMEM((slots, inner), BF16),
            pltpu.VMEM((slots - low, width), BF16),
            pltpu.VMEM((low, 2 * span + 128), BF16),
        ],
        sems=40,
        limit=54,
        flops=12 * slots * width * inner,
        moved=2**24,
    )(got, gated, upper, gate_mat, up_mat, down_mat)
    back = exchange(made)
    layer_out, input_grad = call(
        functools.partial(combine, experts=experts),
        [VMEM] * 9,
        (shape((rows, width), BF16), shape((rows, width), BF16)),
        (VMEM, VMEM),
        limit=48,
        flops=20 * low * rows * width,
        moved=2**23,
    )(back, front, tables, scalars, arrived, stored, cotangent, norm_gain, router_rows)
    return layer_out[None], input_grad[None]


def solution(mesh):
    spread_rows = P("section", "expert", None)
    weights = P("section", "expert", None, None)
    placed = (
        spread_rows,
        spread_rows,
        spread_rows,
        P("section", None),
        P("section", None, None),
        weights,
        weights,
        weights,
        spread_rows,
        spread_rows,
    )
    return jax.shard_map(body, mesh=mesh, in_specs=placed, out_specs=(spread_rows, spread_rows), check_vma=False)
```

```python
import functools

import jax
import jax.numpy as jnp
from jax import lax
from jax.experimental import pallas as pl
from jax.experimental.pallas import tpu as pltpu
from jax.sharding import PartitionSpec as P


NORM_EPS = 1e-06
LOW = 8
HIGH = 4
F32 = jnp.float32
BF16 = jnp.bfloat16
NT = (((1,), (1,)), ((), ()))
ANY = pl.BlockSpec(memory_space=pl.ANY)
HBM = pl.BlockSpec(memory_space=pltpu.HBM)
VMEM = pl.BlockSpec(memory_space=pltpu.VMEM)


def passed_along(value, axis, steps):
    count = lax.axis_size(axis)
    pairs = [(source, (source + steps) % count) for source in range(count)]
    return lax.ppermute(value, axis, pairs)


def mm(a, b):
    return jnp.dot(a, b, preferred_element_type=F32)


def mm_nt(a, b):
    return lax.dot_general(a, b, NT, preferred_element_type=F32)


def iota(shape, dim):
    return lax.broadcasted_iota(jnp.int32, shape, dim)


def mask(condition):
    return condition.astype(F32).astype(BF16)


class Copies:
    def __init__(self, sems):
        self.sems = sems
        self.used = 0

    def start(self, source, target):
        copy = pltpu.make_async_copy(source, target, self.sems.at[self.used])
        self.used += 1
        copy.start()
        return copy


def normalized(tokens, gain_row):
    values = tokens.astype(F32)
    inverse = lax.rsqrt(jnp.mean(values * values, axis=-1, keepdims=True) + NORM_EPS)
    return (values * inverse * gain_row.astype(F32)).astype(BF16), inverse


def places(routes, experts):
    count = routes.shape[1]
    experts_at = iota((experts, count), 0)
    matches = [routes[k : k + 1, :] == experts_at for k in range(2)]
    named = mask(matches[0] | matches[1])
    earlier = mm(named, mask(iota((count, count), 0) < iota((count, count), 1)))
    found = []
    for k in range(2):
        slot = jnp.sum(jnp.where(matches[k], earlier, 0.0), axis=0, keepdims=True).astype(jnp.int32)
        base = routes[k : k + 1, :] * LOW
        whole = jnp.where(slot < LOW, base + slot, -LOW)
        half = jnp.where(slot < LOW, -LOW, base + slot - LOW)
        found.append((whole, half, matches[k]))
    return found


def spots_of(found):
    (w0, h0, _), (w1, h1, _) = found
    return (w0, w1), (h0, h1), (h0 + HIGH, h1 + HIGH)


def table(at, spots, scales=(1.0, 1.0)):
    total = jnp.where(at == spots[0], scales[0], 0.0)
    return total + jnp.where(at == spots[1], scales[1], 0.0)


def pack(tokens, tables, made_ref, out_ref, at, copies):
    whole, left, right = (t.astype(BF16) for t in tables)
    half = tokens.shape[1] // 2
    running = []

    def give(value, column):
        cols = slice(at + column, at + column + half)
        made_ref[:, cols] = value.astype(BF16)
        running.append(copies.start(made_ref.at[:, cols], out_ref.at[:, cols]))

    give(mm(whole, tokens[:, :half]), 0)
    give(mm(whole, tokens[:, half:]), half)
    give(mm(left, tokens[:, :half]) + mm(right, tokens[:, half:]), 2 * half)
    return running


def pack_stored(stored_ref, routes_ref, out_ref, made_ref, sems, *, experts):
    found = places(routes_ref[...], experts)
    at = iota((experts * LOW, routes_ref.shape[1]), 0)
    for copy in pack(stored_ref[...], [table(at, s) for s in spots_of(found)], made_ref, out_ref, 0, Copies(sems)):
        copy.wait()


def weights_of(normed, router_rows, found):
    logits = mm_nt(router_rows, normed)
    sig = [
        jax.nn.sigmoid(jnp.sum(jnp.where(match, logits, 0.0), axis=0, keepdims=True))
        for _, _, match in found
    ]
    total = sig[0] + sig[1]
    return [s / total for s in sig], sig


def split(value):
    high = value.astype(BF16)
    return high, (value - high.astype(F32)).astype(BF16)


def save(kept, tables_ref, span):
    for i, value in enumerate(kept):
        tables_ref[:, i * span : (i + 1) * span] = value.T.astype(BF16)


def prepare_stored(
    stored_ref, gain_ref, router_ref, routes_ref, scaled_ref, tables_ref, scalars_ref, *, experts,
):
    rows = stored_ref.shape[0]
    span = experts * LOW
    at = iota((span, rows), 0)
    normed, inverse = normalized(stored_ref[...], gain_ref[...])
    found = places(routes_ref[...], experts)
    weights, sig = weights_of(normed, router_ref[...], found)
    scales = [w.astype(BF16).astype(F32) for w in weights]
    spots = spots_of(found)
    for i, s in enumerate(spots):
        scaled_ref[:, i * rows : (i + 1) * rows] = table(at, s, scales).astype(BF16)
    kept = [table(at, s) for s in spots]
    kept += [jnp.where(at == s, 1.0, 0.0) for s in (*spots[0], *spots[1])]
    save(kept, tables_ref, span)
    ratio = [jnp.where(s > 0.0, w / s, 1.0) for w, s in zip(weights, scales)]
    routes = routes_ref[...].astype(F32)
    lines = [*weights, *sig, *ratio, routes[0:1], routes[1:2]]
    line_at = iota((rows, rows), 0)
    scalars = jnp.zeros((rows, rows), F32)
    for i, value in enumerate(lines):
        scalars = jnp.where(line_at == i, value, scalars)
    scalars_ref[...] = jnp.where(iota((rows, rows), 1) == len(lines), inverse, scalars.T)


def prepare_front(arrived_ref, gain_ref, router_ref, routes_ref, tables_ref, *, experts):
    rows = arrived_ref.shape[0]
    span = experts * LOW
    at = iota((span, rows), 0)
    normed, _ = normalized(arrived_ref[...], gain_ref[...])
    found = places(routes_ref[...], experts)
    weights, _ = weights_of(normed, router_ref[...], found)
    kept = []
    for s in spots_of(found):
        kept += [part.astype(F32) for part in split(table(at, s, weights))]
    save(kept, tables_ref, span)


def pack_both(
    cotangent_ref, arrived_ref, gain_ref, routes_ref, scaled_ref, out_ref, made_ref, sems, *, experts,
):
    rows, width = arrived_ref.shape
    at = iota((experts * LOW, rows), 0)
    copies = Copies(sems)
    scaled = [scaled_ref[:, i * rows : (i + 1) * rows] for i in range(3)]
    running = pack(cotangent_ref[...], scaled, made_ref, out_ref, 0, copies)
    normed, _ = normalized(arrived_ref[...], gain_ref[...])
    tables = [table(at, s) for s in spots_of(places(routes_ref[...], experts))]
    running += pack(normed, tables, made_ref, out_ref, width + width // 2, copies)
    for copy in running:
        copy.wait()


def half_places(count):
    i = iota((count * HIGH, count * LOW), 0)
    j = iota((count * HIGH, count * LOW), 1)
    left = 2 * i - (i & (HIGH - 1))
    return mask(j == left), mask(j == left + HIGH)


def half_homes(count):
    i = iota((count * LOW, count * HIGH), 1)
    j = iota((count * LOW, count * HIGH), 0)
    left = 2 * i - (i & (HIGH - 1))
    return mask(j == left), mask(j == left + HIGH)


def join_halves(rows_ref, part, sources):
    low = sources * LOW
    half = rows_ref.shape[1] // 2
    take_left, take_right = half_places(sources)
    rows_ref[low:, :half] = mm(take_left, part).astype(BF16)
    rows_ref[low:, half:] = mm(take_right, part).astype(BF16)


def expert_stored(block_ref, gain_ref, gate_ref, up_ref, gated_ref, upper_ref, rows_ref, *, sources):
    low = sources * LOW
    width = rows_ref.shape[1]
    rows_ref[:low, :] = block_ref[:, :width]
    join_halves(rows_ref, block_ref[:, width:], sources)
    for r in range(0, rows_ref.shape[0], 128):
        rows_ref[r : r + 128, :], _ = normalized(rows_ref[r : r + 128, :], gain_ref[...])
    rows = rows_ref[...]
    for f in range(0, gate_ref.shape[1], 256):
        gated_ref[:, f : f + 256] = mm(rows, gate_ref[:, f : f + 256])
        upper_ref[:, f : f + 256] = mm(rows, up_ref[:, f : f + 256])


def expert_both(
    block_any, gated_any, upper_any, gate_any, up_any, down_any, out_any,
    gated_ref, upper_ref, rows_b, half_b, rows_f, half_f, gate_ref, up_ref, down_ref, grad_gate_ref, grad_up_ref, made_ref, out_ref, sems,
    *, sources,
):
    low = sources * LOW
    width = rows_b.shape[1]
    half = width // 2
    span = width + half
    inner = gate_ref.shape[1]
    step = 256
    wide = 512
    copies = Copies(sems)

    def started(source, target, step):
        count = target.shape[0]
        return [copies.start(source.at[i : i + step, :], target.at[i : i + step, :]) for i in range(0, count, step)]

    def taken(running):
        for copy in running:
            copy.wait()

    first = [
        copies.start(block_any.at[:, width:span], half_b),
        copies.start(block_any.at[:, :width], rows_b.at[:low, :]),
        *started(down_any, down_ref, inner // 2),
    ]
    held = [copies.start(gated_any, gated_ref), copies.start(upper_any, upper_ref)]
    taken(first[:2])
    second = started(gate_any, gate_ref, width // 2)
    join_halves(rows_b, half_b[...], sources)
    taken(first[2:])
    second += started(up_any, up_ref, width // 2)
    scores = jnp.zeros((rows_b.shape[0], 1), F32)
    for f in range(0, inner, step):
        cols = slice(f, f + step)
        grad_hidden = mm_nt(rows_b[...], down_ref[cols, :])
        if f == 0:
            taken(held)
        gated = gated_ref[:, cols]
        upper = upper_ref[:, cols]
        sig = jax.nn.sigmoid(gated)
        silu = gated * sig
        hidden = (silu * upper).astype(BF16).astype(F32)
        scores += jnp.sum(grad_hidden * hidden, axis=1, keepdims=True)
        grad_up_ref[:, cols] = (grad_hidden * silu).astype(BF16)
        slope = upper * sig * (1.0 + gated * (1.0 - sig))
        grad_gate_ref[:, cols] = (grad_hidden * slope).astype(BF16)

    put_left, _ = half_homes(sources)
    at = iota((low, 128), 1)
    high, rest = split(scores)
    tail = jnp.where(at == 0, high[:low].astype(F32), jnp.where(at == 1, rest[:low].astype(F32), 0.0))
    at = iota((low // 2, 128), 1)
    more = jnp.where(at == 2, high[low:].astype(F32), jnp.where(at == 3, rest[low:].astype(F32), 0.0))
    out_ref[:, 2 * span :] = (tail + mm(put_left, more.astype(BF16))).astype(BF16)
    given = [copies.start(out_ref.at[:, 2 * span :], out_any.at[:, 2 * span :])]

    def give(columns):
        given.append(copies.start(out_ref.at[:, columns], out_any.at[:, columns]))

    def give_halves(base):
        put_left, put_right = half_homes(sources)
        both = mm(put_left, made_ref[:, :half]) + mm(put_right, made_ref[:, half:])
        out_ref[:, base + width : base + span] = both.astype(BF16)
        give(slice(base + width, base + span))

    taken(second)
    third = [
        copies.start(block_any.at[:, span + width :], half_f),
        copies.start(block_any.at[:, span : span + width], rows_f.at[:low, :]),
    ]
    for n in range(0, width, wide):
        cols = slice(n, n + wide)
        made = (mm_nt(grad_gate_ref[...], gate_ref[cols, :]) + mm_nt(grad_up_ref[...], up_ref[cols, :])).astype(BF16)
        out_ref[:, cols] = made[:low]
        made_ref[:, cols] = made[low:]
        give(cols)
    give_halves(0)

    taken(third)
    join_halves(rows_f, half_f[...], sources)
    for f in range(0, inner, step):
        gate = mm(rows_f[...], gate_ref[:, f : f + step])
        up = mm(rows_f[...], up_ref[:, f : f + step])
        grad_up_ref[:, f : f + step] = (gate * jax.nn.sigmoid(gate) * up).astype(BF16)
    for n in range(0, width, wide):
        made = mm(grad_up_ref[...], down_ref[:, n : n + wide]).astype(BF16)
        cols = slice(span + n, span + n + wide)
        out_ref[:, cols] = made[:low]
        made_ref[:, n : n + wide] = made[low:]
        give(cols)
    give_halves(span)
    for copy in given:
        copy.wait()


def combine(
    back_ref, front_ref, tables_ref, scalars_ref, arrived_ref, stored_ref, cotangent_ref, gain_ref, router_ref,
    layer_ref, grad_ref,
    *, experts,
):
    rows, width = arrived_ref.shape
    half = width // 2
    span = width + half
    slots = experts * LOW

    def t(i):
        return tables_ref[:, i * slots : (i + 1) * slots]

    def w(i):
        return front_ref[:, i * slots : (i + 1) * slots]

    high = back_ref[:, span + width : 2 * span]
    for s, side in ((0, 2), (1, 4)):
        cols = slice(s * half, (s + 1) * half)
        low = back_ref[:, span + s * half : span + (s + 1) * half]
        mixed = mm(w(0), low) + mm(w(1), low) + mm(w(side), high) + mm(w(side + 1), high)
        layer_ref[:, cols] = (arrived_ref[:, cols].astype(F32) + mixed).astype(BF16)

    w0, w1, s0, s1, r0, r1, e0, e1, inverse = (scalars_ref[:, i : i + 1] for i in range(9))
    extra = back_ref[:, 2 * span : 2 * span + 128]
    u = []
    for k, ratio in ((0, r0), (1, r1)):
        got = mm(t(3 + k), extra)
        more = mm(t(5 + k), extra)
        u.append((got[:, 0:1] + got[:, 1:2] + more[:, 2:3] + more[:, 3:4]) * ratio)
    cross = u[0] * w1 - w0 * u[1]
    expert_at = iota((rows, experts), 1).astype(F32)
    picks = jnp.where(e0 == expert_at, cross * (1.0 - s0), 0.0)
    picks = picks - jnp.where(e1 == expert_at, cross * (1.0 - s1), 0.0)
    p0, p1 = split(picks)
    p2 = (picks - p0.astype(F32) - p1.astype(F32)).astype(BF16)
    total = jnp.zeros((rows, 1), F32)
    scaled = []
    high = back_ref[:, width:span]
    for s in range(2):
        cols = slice(s * half, (s + 1) * half)
        grad = mm(t(0), back_ref[:, cols]) + mm(t(1 + s), high)
        router_cols = router_ref[:, cols]
        grad = grad + mm(p0, router_cols) + mm(p1, router_cols) + mm(p2, router_cols)
        grad = grad * gain_ref[:, cols].astype(F32)
        total += jnp.sum(grad * stored_ref[:, cols].astype(F32), axis=1, keepdims=True)
        scaled.append(grad)
    pull = inverse * inverse * inverse * (total / width)
    for s in range(2):
        cols = slice(s * half, (s + 1) * half)
        value = cotangent_ref[:, cols].astype(F32) + inverse * scaled[s]
        grad_ref[:, cols] = (value - stored_ref[:, cols].astype(F32) * pull).astype(BF16)


def call(kernel, ins, outs, out_specs, scratch=(), sems=0, flops=0, moved=0, limit=60):
    return pl.pallas_call(
        kernel,
        in_specs=ins,
        out_specs=out_specs,
        out_shape=outs,
        scratch_shapes=list(scratch) + ([pltpu.SemaphoreType.DMA((sems,))] if sems else []),
        compiler_params=pltpu.CompilerParams(vmem_limit_bytes=limit * 2**20),
        cost_estimate=pl.CostEstimate(flops=flops, bytes_accessed=moved, transcendentals=0),
    )


def body(
    activations, gradients, stashed, norm_gain, router, gate_weight, up_weight, down_weight, routes_forward, routes_backward
):
    shape = jax.ShapeDtypeStruct
    experts = lax.axis_size("expert")
    rows, width = stashed.shape[1:]
    span = width + width // 2
    inner = gate_weight.shape[3]
    low, slots = experts * LOW, experts * (LOW + HIGH)
    gate_mat, up_mat, down_mat = gate_weight[0, 0], up_weight[0, 0], down_weight[0, 0]
    router_rows, stored = router[0].T, stashed[0]
    routes_f, routes_b = routes_forward[0].T, routes_backward[0].T

    def exchange(block):
        blocks = block.reshape(experts, LOW, block.shape[1])
        return lax.all_to_all(blocks, "expert", split_axis=0, concat_axis=0, tiled=True).reshape(block.shape)

    arrived = passed_along(activations, "section", 1)[0]
    cotangent = passed_along(gradients, "section", -1)[0]

    sent_b = call(
        functools.partial(pack_stored, experts=experts),
        [VMEM] * 2,
        shape((low, span), BF16),
        HBM,
        scratch=[pltpu.VMEM((low, span), BF16)],
        sems=3,
        flops=4 * low * rows * width,
        moved=2**22,
    )(stored, routes_b)
    got_b = exchange(sent_b)
    scaled, tables, scalars = call(
        functools.partial(prepare_stored, experts=experts),
        [VMEM] * 4,
        (shape((low, 3 * rows), BF16), shape((rows, 7 * low), BF16), shape((rows, rows), F32)),
        (VMEM,) * 3,
        flops=4 * low * rows * width,
        moved=2**21,
    )(stored, norm_gain, router_rows, routes_b)
    sent = call(
        functools.partial(pack_both, experts=experts),
        [VMEM] * 5,
        shape((low, 2 * span), BF16),
        HBM,
        scratch=[pltpu.VMEM((low, 2 * span), BF16)],
        sems=6,
        flops=10 * low * rows * width,
        moved=2**23,
    )(cotangent, arrived, norm_gain, routes_f, scaled)
    front = call(
        functools.partial(prepare_front, experts=experts),
        [VMEM] * 4,
        shape((rows, 6 * low), BF16),
        VMEM,
        flops=4 * low * rows * width,
        moved=2**21,
    )(arrived, norm_gain, router_rows, routes_f)
    got = exchange(sent)
    gated, upper = call(
        functools.partial(expert_stored, sources=experts),
        [VMEM] * 4,
        (shape((slots, inner), F32), shape((slots, inner), F32)),
        (VMEM, VMEM),
        scratch=[pltpu.VMEM((slots, width), BF16)],
        limit=40,
        flops=4 * slots * width * inner,
        moved=2**24,
    )(got_b, norm_gain, gate_mat, up_mat)
    made = call(
        functools.partial(expert_both, sources=experts),
        [HBM] * 6,
        shape((low, 2 * span + 128), BF16),
        HBM,
        scratch=[
            pltpu.VMEM((slots, inner), F32),
            pltpu.VMEM((slots, inner), F32),
            pltpu.VMEM((slots, width), BF16),
            pltpu.VMEM((low, width // 2), BF16),
            pltpu.VMEM((slots, width), BF16),
            pltpu.VMEM((low, width // 2), BF16),
            pltpu.VMEM((width, inner), BF16),
            pltpu.VMEM((width, inner), BF16),
            pltpu.VMEM((inner, width), BF16),
            pltpu.VMEM((slots, inner), BF16),
            pltpu.VMEM((slots, inner), BF16),
            pltpu.VMEM((slots - low, width), BF16),
            pltpu.VMEM((low, 2 * span + 128), BF16),
        ],
        sems=40,
        limit=54,
        flops=12 * slots * width * inner,
        moved=2**24,
    )(got, gated, upper, gate_mat, up_mat, down_mat)
    back = exchange(made)
    layer_out, input_grad = call(
        functools.partial(combine, experts=experts),
        [VMEM] * 9,
        (shape((rows, width), BF16), shape((rows, width), BF16)),
        (VMEM, VMEM),
        limit=48,
        flops=20 * low * rows * width,
        moved=2**23,
    )(back, front, tables, scalars, arrived, stored, cotangent, norm_gain, router_rows)
    return layer_out[None], input_grad[None]


def solution(mesh):
    spread_rows = P("section", "expert", None)
    weights = P("section", "expert", None, None)
    placed = (
        spread_rows,
        spread_rows,
        spread_rows,
        P("section", None),
        P("section", None, None),
        weights,
        weights,
        weights,
        spread_rows,
        spread_rows,
    )
    return jax.shard_map(body, mesh=mesh, in_specs=placed, out_specs=(spread_rows, spread_rows), check_vma=False)
```
